128 devices in a mesh: pts: 32 (over z, y, core), tile: 4 (over x).
Axes of the slice: x: 4, y: 4, z: 4, core: 2. Of those that a mesh axis runs over, the one named last changes fastest.
Arguments:
- values: float32 [128, 64, 1024], P(('pts', 'tile')), may hold values from -6 to 6
- cycle_taps: float32 [128, 64, 8, 1024], P(('pts', 'tile')), may hold values from 0 to 1
- phi_taps: float32 [128, 64, 8, 1024], P(('pts', 'tile')), may hold values from 0 to 1
- cycle_start: int32 [128, 64, 1024], P(('pts', 'tile')), may hold values from 0 to 24
- phi_start: int32 [128, 64, 1024], P(('pts', 'tile')), may hold values from 0 to 248
- tile_list: int32 [128, 32, 2], replicated, may hold values from 0 to 255, as said below
- response: float32 [4097], replicated, may hold values from 0.05 to 1
Outputs:
- filtered_grid: float32 [256, 32, 8192], P(None, 'tile', 'pts')
- gradient: float32 [128, 64, 1024], P(('pts', 'tile'))
The draws below stay inside these ranges and needn't reach their ends.
Inputs may be any that keep to these rules, and one draw needn't show every extreme that they name: For each point block b and phi column q the 2 entries tile_list[b, q, :] are distinct cycle blocks; slot q * 2 + k of block b holds exactly 1024 points, all of whose taps lie in the tile of cycle block tile_list[b, q, k] and phi column q.
All inputs are finite; a program needn't handle non-finite values.
Results may differ from the reference program's by a relative error of at most 0.0003.
Values sent between devices are 32-bit elements; how exact they have to be, the bound alone decides.
A program may use at most 128 MiB of HBM per device.

```python
import math
import jax
import jax.numpy as jnp
from jax import lax

NPHI = 8192
TR = 32
TAPS = 8
NJ = 256
SLOTS_DEV = 64
PPS = 1024
COLS = 32
BLOCKS = 128
SLOT = 2
TP = 256
FREQS = 4097


def draw_tile_list(key, part):
    scores = jax.random.randint(key, (BLOCKS, COLS, NJ), 0, 1048576, dtype=jnp.int32)
    ranked = scores * NJ + lax.broadcasted_iota(jnp.int32, (BLOCKS, COLS, NJ), 2)
    ordering = jnp.argsort(ranked, axis=-1, stable=True)
    return ordering[:, :, :SLOT].astype(jnp.int32)


def with_ends(values, own_key, least, top_value):
    dims = values.shape
    spot = [jax.random.randint(jax.random.fold_in(own_key, axis), (), 0, dims[axis]) for axis in range(len(dims))]
    values = values.at[tuple(spot)].set(least)
    longest = dims.index(max(dims))
    spot[longest] = (spot[longest] + 1) % dims[longest]
    return values.at[tuple(spot)].set(top_value)


def block_scale(stream_key, extent, shards, smallest, largest):
    gain, own = 1.0, jax.random.fold_in(stream_key, 6)
    for axis_at, shards_of in shards:
        draws = jnp.exp(jax.random.uniform(jax.random.fold_in(own, axis_at), (shards_of,), jnp.float32, smallest / len(shards), largest / len(shards)))
        gain = gain * jnp.repeat(draws, extent[axis_at] // shards_of).reshape([-1 if axis == axis_at else 1 for axis in range(len(extent))])
    return gain


def gaussian(own_key, shape, deviation, limit, pieces=(), kind=jnp.bfloat16):
    entries = deviation * jax.random.normal(own_key, shape, jnp.float32)
    if pieces:
        entries = entries * block_scale(own_key, shape, pieces, -0.22, 0.18)
    return jnp.clip(entries, -limit, limit).astype(kind)


def setup_inputs(seed: int = 0) -> dict:
    splits = jax.random.split(jax.random.key(seed), 8)
    return {
        "values": gaussian(splits[0], (BLOCKS, SLOTS_DEV, PPS), 1.0, 6.0, ((0, 128),), jnp.float32),
        "cycle_taps": jnp.clip(1.0 * jax.random.uniform(splits[1], (BLOCKS, SLOTS_DEV, TAPS, PPS), jnp.float32) ** block_scale(splits[1], (BLOCKS, SLOTS_DEV, TAPS, PPS), ((0, 128),), -0.2, 0.2), 0.0, 1.0),
        "phi_taps": jnp.clip(1.0 * jax.random.uniform(splits[2], (BLOCKS, SLOTS_DEV, TAPS, PPS), jnp.float32) ** block_scale(splits[2], (BLOCKS, SLOTS_DEV, TAPS, PPS), ((0, 128),), -0.2, 0.2), 0.0, 1.0),
        "cycle_start": with_ends(jax.random.randint(splits[3], (BLOCKS, SLOTS_DEV, PPS), 0, TR - TAPS + 1), jax.random.fold_in(splits[3], 1), 0, TR - TAPS).astype(jnp.int32),
        "phi_start": with_ends(jax.random.randint(splits[4], (BLOCKS, SLOTS_DEV, PPS), 0, TP - TAPS + 1), jax.random.fold_in(splits[4], 1), 0, TP - TAPS).astype(jnp.int32),
        "tile_list": draw_tile_list(jax.random.fold_in(splits[7], 71), 0),
        "response": jnp.clip(jnp.exp(jax.random.uniform(splits[6], (FREQS,), jnp.float32, math.log(0.05), math.log(1.0))), 0.05, 1.0),
    }


def cell_layout(block_index, tile_list, cycle_start, phi_start):
    slot_column = jnp.arange(SLOTS_DEV, dtype=jnp.int32) // SLOT
    slot_rank = jnp.arange(SLOTS_DEV, dtype=jnp.int32) % SLOT
    tap_offsets = jnp.arange(TAPS, dtype=jnp.int32)
    listing = tile_list[block_index]
    tile_ids = listing[slot_column, slot_rank].astype(jnp.int32)
    cycle_cells = tile_ids[:, None, None] * TR + cycle_start[block_index][:, None, :] + tap_offsets[None, :, None]
    phi_cells = slot_column[:, None, None] * TP + phi_start[block_index][:, None, :] + tap_offsets[None, :, None]
    return (cycle_cells[:, :, None, :] * NPHI + phi_cells[:, None, :, :]).astype(jnp.int32)


def tap_weights(block_index, cycle_taps, phi_taps):
    return cycle_taps[block_index][:, :, None, :] * phi_taps[block_index][:, None, :, :]


def reference(values, cycle_taps, phi_taps, cycle_start, phi_start, tile_list, response):
    def spread_block(block_index, grid_flat):
        block_index = jnp.asarray(block_index).astype(jnp.int32)
        cell_index = cell_layout(block_index, tile_list, cycle_start, phi_start)
        weight = tap_weights(block_index, cycle_taps, phi_taps) * values[block_index][:, None, None, :]
        return grid_flat.at[cell_index.reshape(-1)].add(weight.reshape(-1))

    grid_flat = lax.fori_loop(0, BLOCKS, spread_block, jnp.zeros((NJ * TR * NPHI,), jnp.float32))
    cycle_rows = grid_flat.reshape(NJ * TR, NPHI)
    spectrum = jnp.fft.rfft(cycle_rows, axis=1) * response[None, :]
    filtered = jnp.fft.irfft(spectrum, n=NPHI, axis=1).astype(jnp.float32)
    filtered_flat = filtered.reshape(-1)

    def read_block(block_index):
        cell_index = cell_layout(block_index, tile_list, cycle_start, phi_start)
        weight = tap_weights(block_index, cycle_taps, phi_taps)
        return jnp.sum(filtered_flat[cell_index] * weight, axis=(1, 2))

    gradient = lax.map(read_block, jnp.arange(BLOCKS, dtype=jnp.int32))
    return filtered.reshape(NJ, TR, NPHI), gradient
```

```python
import functools
import math

import jax
import jax.numpy as jnp
import numpy as np
from jax import lax
from jax.experimental import pallas as pl
from jax.experimental.pallas import tpu as pltpu
from jax.sharding import PartitionSpec as P

NPHI = 8192
TR = 32
NJ = 256
TP = 256
PPS = 1024
COLS = 32
SLOTS_DEV = 64
HALF = COLS // 2 + 1

F32 = jnp.float32
BF16 = jnp.bfloat16
CONTRACT_LAST = (((1,), (1,)), ((), ()))


def split(x):
    high = x.astype(BF16)
    return high, (x - high.astype(F32)).astype(BF16)


def place(taps, start):
    count = taps.shape[1]
    row = lax.broadcasted_iota(jnp.int32, (8, count), 0)
    starts = jnp.broadcast_to(start, (8, count))
    for bit in (1, 2, 4):
        taps = jnp.where((starts & bit) != 0, pltpu.roll(taps, bit, 0), taps)
    return taps, (starts - row + 7) >> 3


def expand(parts, group, groups):
    group = group.astype(F32)
    count = group.shape[1]
    pair = jnp.concatenate([group, group - 1.0], 0).astype(BF16)
    doubled = [jnp.concatenate([part.astype(F32)] * 2, 0).astype(BF16) for part in parts]
    zero = jnp.zeros((16, count), BF16)
    rows = [[] for _ in parts]
    for index in range(groups // 2):
        mask = pair == jnp.asarray(2 * index, BF16)
        for out, part in zip(rows, doubled):
            out.append(jnp.where(mask, part, zero))
    return [jnp.concatenate(out, 0) for out in rows]


def spread_kernel(v_ref, ct_ref, pt_ref, cs_ref, ps_ref, o_ref):
    for s in range(v_ref.shape[0]):
        cycle, cycle_group = place(ct_ref[s] * v_ref[s : s + 1, :], cs_ref[s : s + 1, :])
        phi, phi_group = place(pt_ref[s], ps_ref[s : s + 1, :])
        cycle_high, cycle_low = expand(split(cycle), cycle_group, TR // 8)
        phi_high, phi_low = expand(split(phi), phi_group, TP // 8)
        stacked = jnp.concatenate([cycle_high, cycle_low], 0)
        first = lax.dot_general(phi_high, stacked, CONTRACT_LAST, preferred_element_type=F32)
        second = lax.dot_general(phi_low, cycle_high, CONTRACT_LAST, preferred_element_type=F32)
        tile = (first[:, :TR] + first[:, TR:] + second).T
        o_ref[s // 2, :, s % 2] = tile.reshape(4, 8, TP)


def spread(values, cycle_taps, phi_taps, cycle_start, phi_start, block=8):
    slots = values.shape[0]
    flat = pl.BlockSpec((block, PPS), lambda i: (i, 0))
    taps = pl.BlockSpec((block, 8, PPS), lambda i: (i, 0, 0))
    return pl.pallas_call(
        spread_kernel,
        grid=(slots // block,),
        in_specs=[flat, taps, taps, flat, flat],
        out_specs=pl.BlockSpec((block // 2, 4, 2, 8, TP), lambda i: (i, 0, 0, 0, 0)),
        out_shape=jax.ShapeDtypeStruct((slots // 2, 4, 2, 8, TP), F32),
        name="spread",
    )(values, cycle_taps, phi_taps, cycle_start, phi_start)


def read_kernel(f_ref, ct_ref, pt_ref, cs_ref, ps_ref, o_ref):
    rows = []
    for s in range(ct_ref.shape[0]):
        tile_high, tile_low = split(f_ref[s // 2, :, s % 2].reshape(TR, TP))
        cycle, cycle_group = place(ct_ref[s], cs_ref[s : s + 1, :])
        phi, phi_group = place(pt_ref[s], ps_ref[s : s + 1, :])
        cycle_high, cycle_low = expand(split(cycle), cycle_group, TR // 8)
        right = jnp.concatenate([cycle_high, cycle_low, cycle_high], 0)
        left = jnp.concatenate([tile_high, tile_high, tile_low], 0).T
        along = jnp.dot(left, right, preferred_element_type=F32)
        picked = jnp.zeros((8, PPS), F32)
        for g in range(TP // 8):
            picked = jnp.where(phi_group == g, along[8 * g : 8 * g + 8], picked)
        rows.append(jnp.sum(picked * phi, 0, keepdims=True))
    o_ref[...] = jnp.concatenate(rows, 0)


def read_back(tiles, cycle_taps, phi_taps, cycle_start, phi_start, block=8):
    slots = cycle_taps.shape[0]
    flat = pl.BlockSpec((block, PPS), lambda i: (i, 0))
    taps = pl.BlockSpec((block, 8, PPS), lambda i: (i, 0, 0))
    return pl.pallas_call(
        read_kernel,
        grid=(slots // block,),
        in_specs=[
            pl.BlockSpec((block // 2, 4, 2, 8, TP), lambda i: (i, 0, 0, 0, 0)),
            taps,
            taps,
            flat,
            flat,
        ],
        out_specs=flat,
        out_shape=jax.ShapeDtypeStruct((slots, PPS), F32),
        name="read_back",
    )(tiles, cycle_taps, phi_taps, cycle_start, phi_start)


def accumulate_kernel(j_ref, a_ref, o_ref):
    o_ref[...] = jnp.zeros_like(o_ref)

    def step(i, carry):
        j = j_ref[i]
        o_ref[j] = o_ref[j] + a_ref[i]
        return carry

    lax.fori_loop(0, a_ref.shape[0], step, 0, unroll=8)


def pick_kernel(j_ref, f_ref, o_ref):
    def step(i, carry):
        o_ref[i] = f_ref[j_ref[i]]
        return carry

    lax.fori_loop(0, o_ref.shape[0], step, 0, unroll=8)


def by_index(kernel, name, index, tiles, count):
    vmem = pl.BlockSpec(memory_space=pltpu.VMEM)
    return pl.pallas_call(
        kernel,
        in_specs=[pl.BlockSpec(memory_space=pltpu.SMEM), vmem],
        out_specs=vmem,
        out_shape=jax.ShapeDtypeStruct((count,) + tiles.shape[1:], F32),
        name=name,
    )(index, tiles)


def times(re, im, cos, sin):
    return re * cos - im * sin, re * sin + im * cos


def turn(re, im, angle):
    cos, sin = math.cos(angle), math.sin(angle)
    if abs(sin) < 1e-12:
        return (re, im) if cos > 0 else (-re, -im)
    if abs(cos) < 1e-12:
        return (-im, re) if sin > 0 else (im, -re)
    return re * cos - im * sin, re * sin + im * cos


def real_fft(x):
    n = len(x)
    if n == 1:
        return [(x[0], None)]
    if n == 2:
        return [(x[0] + x[1], None), (x[0] - x[1], None)]
    even, odd = real_fft(x[0::2]), real_fft(x[1::2])
    out = [None] * (n // 2 + 1)
    out[0] = (even[0][0] + odd[0][0], None)
    out[n // 2] = (even[0][0] - odd[0][0], None)
    for k in range(1, n // 4):
        er, ei = even[k]
        tr, ti = turn(odd[k][0], odd[k][1], -2.0 * math.pi * k / n)
        out[k] = (er + tr, ei + ti)
        out[n // 2 - k] = (er - tr, ti - ei)
    quarter = n // 4
    out[quarter] = (even[quarter][0], -odd[quarter][0])
    return out


def real_inverse(spec):
    half = len(spec) - 1
    n = 2 * half
    if n == 2:
        return [spec[0][0] + spec[1][0], spec[0][0] - spec[1][0]]
    even, odd = [None] * (half // 2 + 1), [None] * (half // 2 + 1)
    even[0] = (spec[0][0] + spec[half][0], None)
    odd[0] = (spec[0][0] - spec[half][0], None)
    for k in range(1, half // 2):
        ar, ai = spec[k]
        br, bi = spec[half - k]
        even[k] = (ar + br, ai - bi)
        odd[k] = turn(ar - br, ai + bi, 2.0 * math.pi * k / n)
    middle = half // 2
    even[middle] = (2.0 * spec[middle][0], None)
    odd[middle] = (-2.0 * spec[middle][1], None)
    out = [None] * n
    out[0::2] = real_inverse(even)
    out[1::2] = real_inverse(odd)
    return out


def times_table(rows, table_high, table_low):
    high, low = split(rows)
    dot = functools.partial(jnp.dot, preferred_element_type=F32)
    return dot(high, table_high) + dot(high, table_low) + dot(low, table_high)


def filter_kernel(x_ref, gain_ref, twist_ref, high_ref, low_ref, o_ref):
    cycles = x_ref.shape[1]
    spec = real_fft([x_ref[q] for q in range(COLS)])
    reals, imags = [], []
    for k in range(HALF):
        cos, sin = twist_ref[0, k : k + 1, :], twist_ref[1, k : k + 1, :]
        re, im = spec[k]
        if im is None:
            reals.append(re * cos)
            imags.append(-re * sin)
        else:
            re, im = times(re, im, cos, -sin)
            reals.append(re)
            imags.append(im)
    count = HALF * cycles
    both = times_table(jnp.concatenate(reals + imags, 0), high_ref[...], low_ref[...])
    first, last = both[:count], both[count:]
    freq_re = first[:, :TP] + last[:, TP:]
    freq_im = last[:, :TP] - first[:, TP:]
    gains = [jnp.broadcast_to(gain_ref[k : k + 1, :], (cycles, TP)) for k in range(HALF)]
    gain = jnp.concatenate(gains, 0)
    both = times_table(
        jnp.concatenate([freq_re * gain, freq_im * gain], 0), high_ref[...], low_ref[...]
    )
    first, last = both[:count], both[count:]
    back_re = first[:, :TP] - last[:, TP:]
    back_im = last[:, :TP] + first[:, TP:]
    spec = []
    for k in range(HALF):
        cos, sin = twist_ref[0, k : k + 1, :], twist_ref[1, k : k + 1, :]
        re, im = back_re[k * cycles : (k + 1) * cycles], back_im[k * cycles : (k + 1) * cycles]
        spec.append(times(re, im, cos, sin))
    for q, row in enumerate(real_inverse(spec)):
        o_ref[q] = row


def filter_tables():
    index = np.arange(TP)
    angle = 2.0 * np.pi * (np.outer(index, index) % TP) / TP
    table = np.concatenate([np.cos(angle), np.sin(angle)], 1).astype(np.float32)
    high = table.astype(BF16)
    low = (table - high.astype(np.float32)).astype(BF16)
    angle = 2.0 * np.pi * np.outer(np.arange(HALF), index) / NPHI
    return np.stack([np.cos(angle), np.sin(angle)]).astype(np.float32), high, low


def filter_cycles(cycles, response, block=16):
    count = cycles.shape[1]
    full = jnp.concatenate([response, response[-2:0:-1]]) * (1.0 / NPHI)
    gain = full.reshape(TP, COLS).T[:HALF]
    twist, high, low = filter_tables()
    spec = pl.BlockSpec((COLS, block, TP), lambda i: (0, i, 0))
    whole = lambda *shape: pl.BlockSpec(shape, lambda i: (0,) * len(shape))
    return pl.pallas_call(
        filter_kernel,
        grid=(count // block,),
        in_specs=[spec, whole(HALF, TP), whole(2, HALF, TP), whole(TP, 2 * TP), whole(TP, 2 * TP)],
        out_specs=spec,
        out_shape=jax.ShapeDtypeStruct(cycles.shape, F32),
        name="filter",
    )(cycles, gain, jnp.asarray(twist), jnp.asarray(high), jnp.asarray(low))


def per_device(values, cycle_taps, phi_taps, cycle_start, phi_start, tile_list, response):
    column = lax.axis_index("pts")
    part_count = lax.axis_size("tile")
    points = (cycle_taps[0], phi_taps[0], cycle_start[0], phi_start[0])
    partial = spread(values[0], *points).reshape(COLS * part_count, 2, 8, TP)
    arrived = lax.all_to_all(partial, ("pts", "tile"), split_axis=0, concat_axis=0, tiled=True)
    wanted = lax.dynamic_index_in_dim(tile_list, column, 1, keepdims=False).reshape(-1)
    owned = by_index(accumulate_kernel, "accumulate", wanted, arrived.reshape(-1, 8, TP), NJ)
    cycles = lax.all_to_all(owned, "pts", split_axis=0, concat_axis=0, tiled=True)
    whole = filter_cycles(cycles.reshape(COLS, -1, TP), response)
    filtered = lax.all_to_all(whole, "pts", split_axis=0, concat_axis=0, tiled=True)
    filtered = filtered.reshape(NJ, 8, TP)
    picked = by_index(pick_kernel, "pick", wanted, filtered, wanted.size)
    picked = picked.reshape(COLS * part_count, 2, 8, TP)
    returned = lax.all_to_all(picked, ("pts", "tile"), split_axis=0, concat_axis=0, tiled=True)
    gradient = read_back(returned.reshape(COLS, part_count, 2, 8, TP), *points)
    return filtered, gradient[None]


def solution(mesh):
    return jax.shard_map(
        per_device,
        mesh=mesh,
        in_specs=(
            P(("pts", "tile"), None, None),
            P(("pts", "tile"), None, None, None),
            P(("pts", "tile"), None, None, None),
            P(("pts", "tile"), None, None),
            P(("pts", "tile"), None, None),
            P(),
            P(),
        ),
        out_specs=(P(None, "tile", "pts"), P(("pts", "tile"), None, None)),
        check_vma=False,
    )
```

```python
import functools
import math

import jax
import jax.numpy as jnp
import numpy as np
from jax import lax
from jax.experimental import pallas as pl
from jax.experimental.pallas import tpu as pltpu
from jax.sharding import PartitionSpec as P

NPHI = 8192
TR = 32
NJ = 256
TP = 256
PPS = 1024
COLS = 32
SLOTS_DEV = 64
HALF = COLS // 2 + 1

F32 = jnp.float32
BF16 = jnp.bfloat16
CONTRACT_LAST = (((1,), (1,)), ((), ()))


def split(x):
    high = x.astype(BF16)
    return high, (x - high.astype(F32)).astype(BF16)


def place(taps, start):
    count = taps.shape[1]
    row = lax.broadcasted_iota(jnp.int32, (8, count), 0)
    starts = jnp.broadcast_to(start, (8, count))
    for bit in (1, 2, 4):
        taps = jnp.where((starts & bit) != 0, pltpu.roll(taps, bit, 0), taps)
    return taps, (starts - row + 7) >> 3


def expand(parts, group, groups):
    group = group.astype(F32)
    count = group.shape[1]
    pair = jnp.concatenate([group, group - 1.0], 0).astype(BF16)
    doubled = [jnp.concatenate([part.astype(F32)] * 2, 0).astype(BF16) for part in parts]
    zero = jnp.zeros((16, count), BF16)
    rows = [[] for _ in parts]
    for index in range(groups // 2):
        mask = pair == jnp.asarray(2 * index, BF16)
        for out, part in zip(rows, doubled):
            out.append(jnp.where(mask, part, zero))
    return [jnp.concatenate(out, 0) for out in rows]


MESH = pl.DeviceIdType.MESH
TILES = 4


def spread_tile(values, cycle_taps, phi_taps, cycle_start, phi_start):
    cycle, cycle_group = place(cycle_taps * values, cycle_start)
    phi, phi_group = place(phi_taps, phi_start)
    cycle_high, cycle_low = expand(split(cycle), cycle_group, TR // 8)
    phi_high, phi_low = expand(split(phi), phi_group, TP // 8)
    stacked = jnp.concatenate([cycle_high, cycle_low], 0)
    first = lax.dot_general(phi_high, stacked, CONTRACT_LAST, preferred_element_type=F32)
    second = lax.dot_general(phi_low, cycle_high, CONTRACT_LAST, preferred_element_type=F32)
    return (first[:, :TR] + first[:, TR:] + second).T


def read_tile(tile, cycle_taps, phi_taps, cycle_start, phi_start):
    tile_high, tile_low = split(tile)
    cycle, cycle_group = place(cycle_taps, cycle_start)
    phi, phi_group = place(phi_taps, phi_start)
    cycle_high, cycle_low = expand(split(cycle), cycle_group, TR // 8)
    right = jnp.concatenate([cycle_high, cycle_low, cycle_high], 0)
    left = jnp.concatenate([tile_high, tile_high, tile_low], 0).T
    along = jnp.dot(left, right, preferred_element_type=F32)
    picked = jnp.zeros((8, PPS), F32)
    for g in range(TP // 8):
        picked = jnp.where(phi_group == g, along[8 * g : 8 * g + 8], picked)
    return jnp.sum(picked * phi, 0, keepdims=True)


class Place:
    def __init__(self):
        self.column = lax.axis_index("pts")
        self.part = lax.axis_index("tile")
        self.z = self.column // 8
        self.y = lax.rem(self.column // 2, 4)
        self.core = lax.rem(self.column, 2)

    def offsets(self, i):
        far = lambda k: lax.rem(2 + 3 * k + 3 * (k * (k - 1) // 2), 4)
        a, b = lax.rem(i, 4), lax.rem(i // 4, 4)
        return far(a), far(lax.rem(a + b, 4)), 1 - i // 16

    def target(self, i):
        dz, dy, dc = self.offsets(i)
        z, y = lax.rem(self.z + dz, 4), lax.rem(self.y + dy, 4)
        return (z * 4 + y) * 2 + lax.rem(self.core + dc, 2)

    def source(self, i):
        dz, dy, dc = self.offsets(i)
        z, y = lax.rem(self.z + 4 - dz, 4), lax.rem(self.y + 4 - dy, 4)
        return (z * 4 + y) * 2 + lax.rem(self.core + dc, 2)

    def parts(self, i):
        return [lax.rem(self.part + lax.rem(i, 4) + step, 4) for step in range(TILES)]

    def other(self, column, part):
        return jnp.logical_or(column != self.column, part != self.part)


def greet(here):
    barrier = pltpu.get_barrier_semaphore()

    def step(i, carry):
        column = here.target(i)
        for part in here.parts(i):

            @pl.when(here.other(column, part))
            def _():
                pl.semaphore_signal(
                    barrier, inc=1, device_id=(column, part), device_id_type=MESH
                )

        return carry

    lax.fori_loop(0, COLS, step, 0)
    return barrier


def bytes_of(ref, sem):
    return pltpu.make_async_copy(ref, ref, sem)


def spread_kernel(v_ref, ct_ref, pt_ref, cs_ref, ps_ref, o_ref, stage, send, recv, local):
    here = Place()
    barrier = greet(here)
    me = here.column * TILES + here.part

    def compute(step):
        for half in range(2):
            column = here.target(2 * step + half)
            for k in range(2):
                slot = 2 * column + k
                row = pl.ds(slot, 1)
                tile = spread_tile(
                    v_ref[row, :], ct_ref[slot], pt_ref[slot], cs_ref[row, :], ps_ref[row, :]
                )
                stage[pl.ds(column * TILES, TILES), k] = tile.reshape(TILES, 8, TP)

    def dispatch(step):
        for half in range(2):
            i = 2 * step + half
            column = here.target(i)
            for part in here.parts(i):

                @pl.when(here.other(column, part))
                def _():
                    pltpu.make_async_remote_copy(
                        stage.at[column * TILES + part],
                        o_ref.at[me],
                        send,
                        recv,
                        device_id=(column, part),
                        device_id_type=MESH,
                    ).start()

    compute(0)
    pl.semaphore_wait(barrier, COLS * TILES - 1)

    def step(i, carry):
        compute(i)
        dispatch(i - 1)
        return carry

    lax.fori_loop(1, COLS // 2, step, 0)
    dispatch(COLS // 2 - 1)
    own = pltpu.make_async_copy(stage.at[me], o_ref.at[me], local)
    own.start()
    own.wait()
    others = pl.ds(0, COLS * TILES - 1)
    bytes_of(stage.at[others], send).wait()
    bytes_of(o_ref.at[others], recv).wait()


def spread(values, cycle_taps, phi_taps, cycle_start, phi_start):
    vmem = pl.BlockSpec(memory_space=pltpu.VMEM)
    shape = (COLS * TILES, 2, 8, TP)
    return pl.pallas_call(
        spread_kernel,
        in_specs=[vmem] * 5,
        out_specs=pl.BlockSpec(memory_space=pl.ANY),
        out_shape=jax.ShapeDtypeStruct(shape, F32),
        scratch_shapes=[pltpu.VMEM(shape, F32)] + [pltpu.SemaphoreType.DMA] * 3,
        compiler_params=pltpu.CompilerParams(collective_id=0, has_side_effects=True),
        name="spread",
    )(values, cycle_taps, phi_taps, cycle_start, phi_start)


def accumulate_kernel(j_ref, a_ref, o_ref):
    o_ref[...] = jnp.zeros_like(o_ref)

    def step(i, carry):
        j = j_ref[i]
        o_ref[j] = o_ref[j] + a_ref[i]
        return carry

    lax.fori_loop(0, a_ref.shape[0], step, 0, unroll=8)


def by_index(kernel, name, index, tiles, count):
    vmem = pl.BlockSpec(memory_space=pltpu.VMEM)
    return pl.pallas_call(
        kernel,
        in_specs=[pl.BlockSpec(memory_space=pltpu.SMEM), vmem],
        out_specs=vmem,
        out_shape=jax.ShapeDtypeStruct((count,) + tiles.shape[1:], F32),
        name=name,
    )(index, tiles)


def times(re, im, cos, sin):
    return re * cos - im * sin, re * sin + im * cos


def turn(re, im, angle):
    cos, sin = math.cos(angle), math.sin(angle)
    if abs(sin) < 1e-12:
        return (re, im) if cos > 0 else (-re, -im)
    if abs(cos) < 1e-12:
        return (-im, re) if sin > 0 else (im, -re)
    return re * cos - im * sin, re * sin + im * cos


def real_fft(x):
    n = len(x)
    if n == 1:
        return [(x[0], None)]
    if n == 2:
        return [(x[0] + x[1], None), (x[0] - x[1], None)]
    even, odd = real_fft(x[0::2]), real_fft(x[1::2])
    out = [None] * (n // 2 + 1)
    out[0] = (even[0][0] + odd[0][0], None)
    out[n // 2] = (even[0][0] - odd[0][0], None)
    for k in range(1, n // 4):
        er, ei = even[k]
        tr, ti = turn(odd[k][0], odd[k][1], -2.0 * math.pi * k / n)
        out[k] = (er + tr, ei + ti)
        out[n // 2 - k] = (er - tr, ti - ei)
    quarter = n // 4
    out[quarter] = (even[quarter][0], -odd[quarter][0])
    return out


def real_inverse(spec):
    half = len(spec) - 1
    n = 2 * half
    if n == 2:
        return [spec[0][0] + spec[1][0], spec[0][0] - spec[1][0]]
    even, odd = [None] * (half // 2 + 1), [None] * (half // 2 + 1)
    even[0] = (spec[0][0] + spec[half][0], None)
    odd[0] = (spec[0][0] - spec[half][0], None)
    for k in range(1, half // 2):
        ar, ai = spec[k]
        br, bi = spec[half - k]
        even[k] = (ar + br, ai - bi)
        odd[k] = turn(ar - br, ai + bi, 2.0 * math.pi * k / n)
    middle = half // 2
    even[middle] = (2.0 * spec[middle][0], None)
    odd[middle] = (-2.0 * spec[middle][1], None)
    out = [None] * n
    out[0::2] = real_inverse(even)
    out[1::2] = real_inverse(odd)
    return out


def times_table(rows, table_high, table_low):
    high, low = split(rows)
    dot = functools.partial(jnp.dot, preferred_element_type=F32)
    return dot(high, table_high) + dot(high, table_low) + dot(low, table_high)


def filter_rows(rows, gain_ref, twist_ref, high_ref, low_ref):
    cycles = rows[0].shape[0]
    spec = real_fft(rows)
    reals, imags = [], []
    for k in range(HALF):
        cos, sin = twist_ref[0, k : k + 1, :], twist_ref[1, k : k + 1, :]
        re, im = spec[k]
        if im is None:
            reals.append(re * cos)
            imags.append(-re * sin)
        else:
            re, im = times(re, im, cos, -sin)
            reals.append(re)
            imags.append(im)
    count = HALF * cycles
    both = times_table(jnp.concatenate(reals + imags, 0), high_ref[...], low_ref[...])
    first, last = both[:count], both[count:]
    freq_re = first[:, :TP] + last[:, TP:]
    freq_im = last[:, :TP] - first[:, TP:]
    gains = [jnp.broadcast_to(gain_ref[k : k + 1, :], (cycles, TP)) for k in range(HALF)]
    gain = jnp.concatenate(gains, 0)
    both = times_table(
        jnp.concatenate([freq_re * gain, freq_im * gain], 0), high_ref[...], low_ref[...]
    )
    first, last = both[:count], both[count:]
    back_re = first[:, :TP] - last[:, TP:]
    back_im = last[:, :TP] + first[:, TP:]
    spec = []
    for k in range(HALF):
        cos, sin = twist_ref[0, k : k + 1, :], twist_ref[1, k : k + 1, :]
        re, im = back_re[k * cycles : (k + 1) * cycles], back_im[k * cycles : (k + 1) * cycles]
        spec.append(times(re, im, cos, sin))
    return real_inverse(spec)


def filter_tables():
    index = np.arange(TP)
    angle = 2.0 * np.pi * (np.outer(index, index) % TP) / TP
    table = np.concatenate([np.cos(angle), np.sin(angle)], 1).astype(np.float32)
    high = table.astype(BF16)
    low = (table - high.astype(np.float32)).astype(BF16)
    angle = 2.0 * np.pi * np.outer(np.arange(HALF), index) / NPHI
    return np.stack([np.cos(angle), np.sin(angle)]).astype(np.float32), high, low


CHUNKS = 4
CHUNK_J = 2


def filter_kernel(
    j_ref, owned_ref, gain_ref, twist_ref, high_ref, low_ref, ct_hbm, pt_hbm, cs_hbm, ps_hbm,
    filtered_ref, gradient_ref,
    ct_ref, pt_ref, cs_ref, ps_ref, arrived, ready, filtered, picked, returned,
    load_sem, out_sem, send_in, recv_in, own_in, send_out, recv_out, own_out,
    send_pick, recv_pick, own_pick,
):
    here = Place()
    barrier = greet(here)
    me, mine = here.column, here.part
    loads = [
        pltpu.make_async_copy(source, target, load_sem.at[n])
        for n, (source, target) in enumerate(
            [(ct_hbm, ct_ref), (pt_hbm, pt_ref), (cs_hbm, cs_ref), (ps_hbm, ps_ref)]
        )
    ]

    def rows_of(column, chunk):
        return pl.ds(column * (CHUNKS * CHUNK_J) + chunk * CHUNK_J, CHUNK_J)

    def own_row(chunk):
        return pltpu.make_async_copy(
            owned_ref.at[rows_of(me, chunk)], arrived.at[chunk, me], own_in.at[chunk]
        )

    for chunk in range(CHUNKS):
        own_row(chunk).start()
    pl.semaphore_wait(barrier, COLS * TILES - 1)

    def send_rows(n, carry):
        chunk, i = n // COLS, lax.rem(n, COLS)
        column = here.target(i)

        @pl.when(column != me)
        def _():
            pltpu.make_async_remote_copy(
                owned_ref.at[rows_of(column, chunk)],
                arrived.at[chunk, me],
                send_in,
                recv_in.at[chunk],
                device_id=(column, mine),
                device_id_type=MESH,
            ).start()

        return carry

    lax.fori_loop(0, CHUNKS * COLS, send_rows, 0)
    for load in loads:
        load.start()

    def filter_chunk(chunk, carry):
        bytes_of(arrived.at[chunk, pl.ds(0, COLS - 1)], recv_in.at[chunk]).wait()
        own_row(chunk).wait()
        rows = [arrived[chunk, q].reshape(CHUNK_J * 8, TP) for q in range(COLS)]
        rows = filter_rows(rows, gain_ref, twist_ref, high_ref, low_ref)
        for q in range(COLS):
            ready[chunk, q] = rows[q].reshape(CHUNK_J, 8, TP)

        def send_ready(i, carry):
            column = here.target(i)

            @pl.when(column != me)
            def _():
                pltpu.make_async_remote_copy(
                    ready.at[chunk, column],
                    filtered.at[rows_of(me, chunk)],
                    send_out,
                    recv_out,
                    device_id=(column, mine),
                    device_id_type=MESH,
                ).start()

            return carry

        lax.fori_loop(0, COLS, send_ready, 0)
        pltpu.make_async_copy(
            ready.at[chunk, me], filtered.at[rows_of(me, chunk)], own_out.at[chunk]
        ).start()
        return carry

    lax.fori_loop(0, CHUNKS, filter_chunk, 0)
    for chunk in range(CHUNKS):
        pltpu.make_async_copy(
            ready.at[chunk, me], filtered.at[rows_of(me, chunk)], own_out.at[chunk]
        ).wait()
    bytes_of(filtered.at[pl.ds(0, NJ - CHUNKS * CHUNK_J)], recv_out).wait()
    store = pltpu.make_async_copy(filtered, filtered_ref, out_sem)
    store.start()

    def pick_and_send(i, carry):
        column = here.target(i)
        for part in range(TILES):
            block = column * TILES + part
            for k in range(2):
                picked[block, k] = filtered[j_ref[2 * block + k]]
        for part in here.parts(i):

            @pl.when(here.other(column, part))
            def _():
                pltpu.make_async_remote_copy(
                    picked.at[column * TILES + part],
                    returned.at[me, mine],
                    send_pick,
                    recv_pick.at[me],
                    device_id=(column, part),
                    device_id_type=MESH,
                ).start()

        return carry

    lax.fori_loop(0, COLS, pick_and_send, 0)
    own = pltpu.make_async_copy(picked.at[me * TILES + mine], returned.at[me, mine], own_pick)
    own.start()
    for load in loads:
        load.wait()
    own.wait()

    def read(i, carry):
        column = here.source(i)

        @pl.when(column != me)
        def _():
            bytes_of(returned.at[column], recv_pick.at[column]).wait()

        @pl.when(column == me)
        def _():
            bytes_of(returned.at[column, pl.ds(0, TILES - 1)], recv_pick.at[column]).wait()

        for k in range(2):
            slot = 2 * column + k
            row = pl.ds(slot, 1)
            gradient_ref[row, :] = read_tile(
                returned[column, :, k].reshape(TR, TP),
                ct_ref[slot],
                pt_ref[slot],
                cs_ref[row, :],
                ps_ref[row, :],
            )
        return carry

    lax.fori_loop(0, COLS, read, 0)
    bytes_of(arrived.at[:, pl.ds(0, COLS - 1)], send_in).wait()
    bytes_of(ready.at[:, pl.ds(0, COLS - 1)], send_out).wait()
    bytes_of(picked.at[pl.ds(0, COLS * TILES - 1)], send_pick).wait()
    store.wait()


def filter_and_read(wanted, owned, response, cycle_taps, phi_taps, cycle_start, phi_start):
    full = jnp.concatenate([response, response[-2:0:-1]]) * (1.0 / NPHI)
    gain = full.reshape(TP, COLS).T[:HALF]
    twist, high, low = filter_tables()
    vmem = pl.BlockSpec(memory_space=pltpu.VMEM)
    hbm = pl.BlockSpec(memory_space=pl.ANY)
    tiles = (COLS * TILES, 2, 8, TP)
    blocks = (CHUNKS, COLS, CHUNK_J, 8, TP)
    dma = pltpu.SemaphoreType.DMA
    return pl.pallas_call(
        filter_kernel,
        in_specs=[pl.BlockSpec(memory_space=pltpu.SMEM), hbm] + [vmem] * 4 + [hbm] * 4,
        out_specs=(hbm, vmem),
        out_shape=(
            jax.ShapeDtypeStruct((NJ, 8, TP), F32),
            jax.ShapeDtypeStruct((SLOTS_DEV, PPS), F32),
        ),
        scratch_shapes=[
            pltpu.VMEM(cycle_taps.shape, F32),
            pltpu.VMEM(phi_taps.shape, F32),
            pltpu.VMEM(cycle_start.shape, jnp.int32),
            pltpu.VMEM(phi_start.shape, jnp.int32),
            pltpu.VMEM(blocks, F32),
            pltpu.VMEM(blocks, F32),
            pltpu.VMEM((NJ, 8, TP), F32),
            pltpu.VMEM(tiles, F32),
            pltpu.VMEM((COLS, TILES, 2, 8, TP), F32),
            dma((4,)),
            dma,
            dma,
            dma((CHUNKS,)),
            dma((CHUNKS,)),
            dma,
            dma,
            dma((CHUNKS,)),
            dma,
            dma((COLS,)),
            dma,
        ],
        compiler_params=pltpu.CompilerParams(
            collective_id=1, has_side_effects=True, vmem_limit_bytes=48 << 20
        ),
        name="filter_and_read",
    )(
        wanted,
        owned,
        gain,
        jnp.asarray(twist),
        jnp.asarray(high),
        jnp.asarray(low),
        cycle_taps,
        phi_taps,
        cycle_start,
        phi_start,
    )


def per_device(values, cycle_taps, phi_taps, cycle_start, phi_start, tile_list, response):
    points = (cycle_taps[0], phi_taps[0], cycle_start[0], phi_start[0])
    arrived = spread(values[0], *points)
    column = lax.axis_index("pts")
    wanted = lax.dynamic_index_in_dim(tile_list, column, 1, keepdims=False).reshape(-1)
    owned = by_index(accumulate_kernel, "accumulate", wanted, arrived.reshape(-1, 8, TP), NJ)
    filtered, gradient = filter_and_read(wanted, owned, response, *points)
    return filtered, gradient[None]


def solution(mesh):
    return jax.shard_map(
        per_device,
        mesh=mesh,
        in_specs=(
            P(("pts", "tile"), None, None),
            P(("pts", "tile"), None, None, None),
            P(("pts", "tile"), None, None, None),
            P(("pts", "tile"), None, None),
            P(("pts", "tile"), None, None),
            P(),
            P(),
        ),
        out_specs=(P(None, "tile", "pts"), P(("pts", "tile"), None, None)),
        check_vma=False,
    )
```

```python
import functools
import math

import jax
import jax.numpy as jnp
import numpy as np
from jax import lax
from jax.experimental import pallas as pl
from jax.experimental.pallas import tpu as pltpu
from jax.sharding import PartitionSpec as P

NPHI = 8192
TR = 32
NJ = 256
TP = 256
PPS = 1024
COLS = 32
SLOTS_DEV = 64
HALF = COLS // 2 + 1
HALF_TP = TP // 2

F32 = jnp.float32
BF16 = jnp.bfloat16
CONTRACT_LAST = (((1,), (1,)), ((), ()))


def split(x):
    high = x.astype(BF16)
    return high, (x - high.astype(F32)).astype(BF16)


def place(taps, start):
    count = taps.shape[1]
    row = lax.broadcasted_iota(jnp.int32, (8, count), 0)
    starts = jnp.broadcast_to(start, (8, count))
    for bit in (1, 2, 4):
        taps = jnp.where((starts & bit) != 0, pltpu.roll(taps, bit, 0), taps)
    return taps, (starts - row + 7) >> 3


def expand(parts, group, groups, first=0):
    group = group.astype(F32)
    count = group.shape[1]
    pair = jnp.concatenate([group, group - 1.0], 0).astype(BF16)
    doubled = [jnp.concatenate([part.astype(F32)] * 2, 0).astype(BF16) for part in parts]
    zero = jnp.zeros((16, count), BF16)
    rows = [[] for _ in parts]
    for index in range(groups // 2):
        mask = pair == jnp.asarray(2 * index + first, BF16)
        for out, part in zip(rows, doubled):
            out.append(jnp.where(mask, part, zero))
    return [jnp.concatenate(out, 0) for out in rows]


MESH = pl.DeviceIdType.MESH
TILES = 4
FAR_FIRST = (2, 1, 3, 0)
STEPS = COLS // 4
SELF_STEP = 5


def spread_tile(half, values, cycle_taps, phi_taps, cycle_start, phi_start):
    cycle, cycle_group = place(cycle_taps * values, cycle_start)
    phi, phi_group = place(phi_taps, phi_start)
    cycle_high, cycle_low = expand(split(cycle), cycle_group, TR // 8)
    phi_high, phi_low = expand(split(phi), phi_group, HALF_TP // 8, half * (HALF_TP // 8))
    stacked = jnp.concatenate([cycle_high, cycle_low], 0)
    first = lax.dot_general(phi_high, stacked, CONTRACT_LAST, preferred_element_type=F32)
    second = lax.dot_general(phi_low, cycle_high, CONTRACT_LAST, preferred_element_type=F32)
    return (first[:, :TR] + first[:, TR:] + second).T


def read_tile(tile, cycle_taps, phi_taps, cycle_start, phi_start):
    tile_high, tile_low = split(tile)
    cycle, cycle_group = place(cycle_taps, cycle_start)
    phi, phi_group = place(phi_taps, phi_start)
    cycle_high, cycle_low = expand(split(cycle), cycle_group, TR // 8)
    right = jnp.concatenate([cycle_high, cycle_low, cycle_high], 0)
    left = jnp.concatenate([tile_high, tile_high, tile_low], 0).T
    along = jnp.dot(left, right, preferred_element_type=F32)
    picked = jnp.zeros((8, PPS), F32)
    for g in range(TP // 8):
        picked = jnp.where(phi_group == g, along[8 * g : 8 * g + 8], picked)
    return jnp.sum(picked * phi, 0, keepdims=True)


class Place:
    def __init__(self):
        self.column = lax.axis_index("pts")
        self.part = lax.axis_index("tile")
        z, self.y = self.column // 8, lax.rem(self.column // 2, 4)
        self.core = lax.rem(self.column, 2)
        self.ahead = [lax.rem(z + dz, 4) * 8 for dz in FAR_FIRST]
        self.behind = [lax.rem(z + 4 - dz, 4) * 8 for dz in FAR_FIRST]
        self.parts = [lax.rem(self.part + dx, 4) for dx in FAR_FIRST]

    def core_at(self, step):
        return lax.rem(self.core + 1 + step // 4, 2)

    def target(self, step, n):
        return self.ahead[n] + 2 * lax.rem(self.y + step + n, 4) + self.core_at(step)

    def source(self, step, n):
        return self.behind[n] + 2 * lax.rem(self.y + 16 - step - n, 4) + self.core_at(step)


def unless_self(step, n, action):
    if n != 3:
        action()
    elif isinstance(step, int):
        if step != SELF_STEP:
            action()
    else:
        pl.when(step != SELF_STEP)(action)


def greet(here):
    barrier = pltpu.get_barrier_semaphore()
    for step in range(STEPS):
        for n in range(4):
            column = here.target(step, n)
            for dx, part in zip(FAR_FIRST, here.parts):
                if (step, n, dx) != (SELF_STEP, 3, 0):
                    pl.semaphore_signal(
                        barrier, inc=1, device_id=(column, part), device_id_type=MESH
                    )
    return barrier


def bytes_of(ref, sem):
    return pltpu.make_async_copy(ref, ref, sem)


def times(re, im, cos, sin):
    return re * cos - im * sin, re * sin + im * cos


def turn(re, im, angle):
    cos, sin = math.cos(angle), math.sin(angle)
    if abs(sin) < 1e-12:
        return (re, im) if cos > 0 else (-re, -im)
    if abs(cos) < 1e-12:
        return (-im, re) if sin > 0 else (im, -re)
    return re * cos - im * sin, re * sin + im * cos


def real_fft(x):
    n = len(x)
    if n == 1:
        return [(x[0], None)]
    if n == 2:
        return [(x[0] + x[1], None), (x[0] - x[1], None)]
    even, odd = real_fft(x[0::2]), real_fft(x[1::2])
    out = [None] * (n // 2 + 1)
    out[0] = (even[0][0] + odd[0][0], None)
    out[n // 2] = (even[0][0] - odd[0][0], None)
    for k in range(1, n // 4):
        er, ei = even[k]
        tr, ti = turn(odd[k][0], odd[k][1], -2.0 * math.pi * k / n)
        out[k] = (er + tr, ei + ti)
        out[n // 2 - k] = (er - tr, ti - ei)
    quarter = n // 4
    out[quarter] = (even[quarter][0], -odd[quarter][0])
    return out


def real_inverse(spec):
    half = len(spec) - 1
    n = 2 * half
    if n == 2:
        return [spec[0][0] + spec[1][0], spec[0][0] - spec[1][0]]
    even, odd = [None] * (half // 2 + 1), [None] * (half // 2 + 1)
    even[0] = (spec[0][0] + spec[half][0], None)
    odd[0] = (spec[0][0] - spec[half][0], None)
    for k in range(1, half // 2):
        ar, ai = spec[k]
        br, bi = spec[half - k]
        even[k] = (ar + br, ai - bi)
        odd[k] = turn(ar - br, ai + bi, 2.0 * math.pi * k / n)
    middle = half // 2
    even[middle] = (2.0 * spec[middle][0], None)
    odd[middle] = (-2.0 * spec[middle][1], None)
    out = [None] * n
    out[0::2] = real_inverse(even)
    out[1::2] = real_inverse(odd)
    return out


def times_table(rows, table_high, table_low):
    high, low = split(rows)
    dot = functools.partial(jnp.dot, preferred_element_type=F32)
    return dot(high, table_high) + dot(high, table_low) + dot(low, table_high)


def filter_rows(rows, gain_ref, twist_ref, tables):
    cycles = rows[0].shape[0]
    spec = real_fft(rows)
    reals, imags = [], []
    for k in range(HALF):
        cos, sin = twist_ref[0, k : k + 1, :], twist_ref[1, k : k + 1, :]
        re, im = spec[k]
        if im is None:
            reals.append(re * cos)
            imags.append(-re * sin)
        else:
            re, im = times(re, im, cos, -sin)
            reals.append(re)
            imags.append(im)
    count = HALF * cycles
    both = times_table(jnp.concatenate(reals + imags, 0), tables[0], tables[1])
    first, last = both[:count], both[count:]
    freq_re = first[:, :TP] + last[:, TP:]
    freq_im = last[:, :TP] - first[:, TP:]
    gains = [jnp.broadcast_to(gain_ref[k : k + 1, :], (cycles, TP)) for k in range(HALF)]
    gain = jnp.concatenate(gains, 0)
    both = times_table(
        jnp.concatenate([freq_re * gain, freq_im * gain], 0), tables[2], tables[3]
    )
    first, last = both[:count], both[count:]
    back_re = first[:, :TP] - last[:, TP:]
    back_im = last[:, :TP] + first[:, TP:]
    spec = []
    for k in range(HALF):
        cos, sin = twist_ref[0, k : k + 1, :], twist_ref[1, k : k + 1, :]
        re, im = back_re[k * cycles : (k + 1) * cycles], back_im[k * cycles : (k + 1) * cycles]
        spec.append(times(re, im, cos, sin))
    return real_inverse(spec)


def filter_tables():
    index = np.arange(TP)
    low_half = 4 * (np.arange(HALF_TP) % COLS) + np.arange(HALF_TP) // COLS
    order = np.concatenate([low_half, TP - 1 - low_half])
    angle = 2.0 * np.pi * (np.outer(index, order) % TP) / TP
    tables = []
    for cos, sin in [(np.cos(angle), np.sin(angle)), (np.cos(angle).T, np.sin(angle).T)]:
        table = np.concatenate([cos, sin], 1).astype(np.float32)
        high = table.astype(BF16)
        tables += [high, (table - high.astype(np.float32)).astype(BF16)]
    angle = 2.0 * np.pi * np.outer(np.arange(HALF), index) / NPHI
    return np.stack([np.cos(angle), np.sin(angle)]).astype(np.float32), np.stack(tables)


def gain_table(response_ref):
    rows = [response_ref[HALF_TP * s : HALF_TP * (s + 1)].reshape(1, HALF_TP) for s in range(COLS)]
    turned = jnp.concatenate(rows, 0).T
    grid = jnp.concatenate([turned[COLS * b : COLS * (b + 1)] for b in range(4)], 1)
    lane = lax.broadcasted_iota(jnp.int32, (8, HALF_TP), 1)
    zeroth = jnp.broadcast_to(grid[:1], (8, HALF_TP))
    ahead = jnp.where(
        lane < 3 * COLS, pltpu.roll(zeroth, 3 * COLS, 1), pltpu.roll(zeroth, 3 * COLS - 1, 1)
    )
    last = response_ref[NPHI // 2 : NPHI // 2 + 1].reshape(1, 1)
    ahead = jnp.where(lane == HALF_TP - 1, jnp.broadcast_to(last, (8, HALF_TP)), ahead)
    mirrored = [ahead[:1]] + [grid[COLS - k : COLS - k + 1] for k in range(1, HALF)]
    both = jnp.concatenate([grid[:HALF], jnp.concatenate(mirrored, 0)], 1)
    return both * (1.0 / NPHI)


def same_block_links(wanted):
    lane = lax.broadcasted_iota(jnp.int32, (HALF_TP, HALF_TP), 1)
    across = [jnp.broadcast_to(wanted[k : k + 1], (HALF_TP, HALF_TP)) for k in range(2)]
    down = [x.T for x in across]
    item = [2 * lax.broadcasted_iota(jnp.int32, (HALF_TP, HALF_TP), 0) + k for k in range(2)]

    def latest(matches):
        found = [
            jnp.max(jnp.where(match, item[k], -1), 0, keepdims=True)
            for k, match in enumerate(matches)
        ]
        found = jnp.maximum(found[0], found[1])
        return jnp.where(found < 0, NJ, found)

    links = []
    for k in range(2):
        here = 2 * lane + k
        links.append(
            latest([jnp.logical_and(down[n] == across[k], item[n] < here) for n in range(2)])
        )
    for half in range(2):
        links.append(latest([down[n] == lane + HALF_TP * half for n in range(2)]))
    return links


def within(entry):
    return jnp.minimum(jnp.maximum(entry, 0), NJ)


CHUNKS = 4
CHUNK_J = 2
GROUP_J = CHUNKS * CHUNK_J


def whole_kernel(
    list_smem, list_vmem, v_ref, ct_ref, pt_ref, cs_ref, ps_ref,
    response_ref, twist_ref, table_ref,
    filtered_ref, gradient_ref,
    links_vmem, links, gain_ref, stage, arrived0, arrived1, owned, rows0, rows1,
    ready, filtered0, filtered1, picked, returned,
    links_sem, out_sem, send_tile, recv_tile, own_tile,
    send_row, recv_row0, recv_row1, own_row, send_out, recv_out, own_out,
    send_pick, recv_pick, own_pick,
):
    here = Place()
    barrier = greet(here)
    column_me, part_me = here.column, here.part
    me = column_me * TILES + part_me
    arrived, filtered = (arrived0, arrived1), (filtered0, filtered1)
    others = COLS * TILES - 1

    def each_other(step, n, action):
        column = here.target(step, n)
        for dx, part in zip(FAR_FIRST, here.parts):
            send = functools.partial(action, column, part)
            if dx:
                send()
            else:
                unless_self(step, n, send)

    def each_column(action):
        def visit(step, carry):
            for n in range(4):
                unless_self(step, n, functools.partial(action, here.target(step, n)))
            return carry

        lax.fori_loop(0, STEPS, visit, 0)

    def remote(source, target, sent, received, column, part):
        pltpu.make_async_remote_copy(
            source, target, sent, received, device_id=(column, part), device_id_type=MESH
        ).start()

    for n, link in enumerate(same_block_links(list_vmem[column_me])):
        links_vmem[n : n + 1, :] = link
    gain_ref[...] = gain_table(response_ref)
    for half in range(2):
        arrived[half][NJ] = jnp.zeros((8, HALF_TP), F32)

    def compute(half, step):
        for n in range(4):
            column = here.target(step, n)
            for k in range(2):
                slot = 2 * column + k
                row = pl.ds(slot, 1)
                tile = spread_tile(
                    half, v_ref[row, :], ct_ref[slot], pt_ref[slot], cs_ref[row, :], ps_ref[row, :]
                )
                stage[half, pl.ds(column * TILES, TILES), k] = tile.reshape(TILES, 8, HALF_TP)

    def dispatch(half, step):
        def send(column, part):
            remote(
                stage.at[half, column * TILES + part],
                arrived[half].at[pl.ds(2 * me, 2)],
                send_tile,
                recv_tile.at[half],
                column,
                part,
            )

        for n in range(4):
            each_other(step, n, send)

    def own_tiles(half):
        return pltpu.make_async_copy(
            stage.at[half, me], arrived[half].at[pl.ds(2 * me, 2)], own_tile.at[half]
        )

    copy_links = pltpu.make_async_copy(links_vmem, links, links_sem)
    compute(0, 0)
    copy_links.start()
    pl.semaphore_wait(barrier, others)
    for half in range(2):

        def spread_step(step, carry):
            compute(half, step)
            dispatch(half, step - 1)
            return carry

        if half:
            compute(half, 0)
            dispatch(0, STEPS - 1)
            own_tiles(0).start()
        lax.fori_loop(1, STEPS, spread_step, 0)
    dispatch(1, STEPS - 1)
    own_tiles(1).start()
    copy_links.wait()

    for half in range(2):
        tiles = arrived[half]
        bytes_of(tiles.at[pl.ds(0, 2 * others)], recv_tile.at[half]).wait()
        own_tiles(half).wait()

        def add(b, carry):
            for k in range(2):
                tiles[2 * b + k] = tiles[2 * b + k] + tiles[within(links[k, b])]
            return carry

        lax.fori_loop(0, COLS * TILES, add, 0, unroll=4)

        def gather(column):
            first = column // 16
            for j in range(GROUP_J):
                entry = links[2 + first, (column - 16 * first) * GROUP_J + j]
                owned[half, column * GROUP_J + j] = tiles[within(entry)]

        if half == 0:

            def send_rows(column):
                remote(
                    owned.at[0, pl.ds(column * GROUP_J, GROUP_J)],
                    rows0.at[column_me],
                    send_row,
                    recv_row0,
                    column,
                    part_me,
                )

            def row_step(step, carry):
                for n in range(4):
                    gather(here.target(step, n))
                for n in range(4):
                    column = here.target(step - 1, n)
                    unless_self(step - 1, n, functools.partial(send_rows, column))
                return carry

            for n in range(4):
                gather(here.target(0, n))
            lax.fori_loop(1, STEPS, row_step, 0)
            for n in range(4):
                send_rows(here.target(STEPS - 1, n))
        else:

            def row_step(step, carry):
                for n in range(4):
                    gather(here.target(step, n))
                return carry

            lax.fori_loop(0, STEPS, row_step, 0)

            def send_chunk(chunk, carry):
                def send(column):
                    remote(
                        owned.at[1, pl.ds(column * GROUP_J + chunk * CHUNK_J, CHUNK_J)],
                        rows1.at[chunk, column_me],
                        send_row,
                        recv_row1.at[chunk],
                        column,
                        part_me,
                    )

                each_column(send)
                return carry

            lax.fori_loop(0, CHUNKS, send_chunk, 0)

    own_rows = [
        pltpu.make_async_copy(
            owned.at[0, pl.ds(column_me * GROUP_J, GROUP_J)], rows0.at[column_me], own_row.at[0]
        )
    ]
    for chunk in range(CHUNKS):
        own_rows.append(
            pltpu.make_async_copy(
                owned.at[1, pl.ds(column_me * GROUP_J + chunk * CHUNK_J, CHUNK_J)],
                rows1.at[chunk, column_me],
                own_row.at[1 + chunk],
            )
        )
    for copy in own_rows:
        copy.start()
    for copy in own_rows:
        copy.wait()
    bytes_of(rows0.at[pl.ds(0, COLS - 1)], recv_row0).wait()

    def chunk_rows(chunk):
        return pl.ds(column_me * GROUP_J + chunk * CHUNK_J, CHUNK_J)

    def own_ready(half, chunk):
        return pltpu.make_async_copy(
            ready.at[half, chunk, column_me],
            filtered[half].at[chunk_rows(chunk)],
            own_out.at[half, chunk],
        )

    def send_ready(half, chunk):
        def send(column):
            remote(
                ready.at[half, chunk, column],
                filtered[half].at[chunk_rows(chunk)],
                send_out,
                recv_out.at[half],
                column,
                part_me,
            )

        each_column(send)
        own_ready(half, chunk).start()

    def filter_chunk(chunk, carry):
        bytes_of(rows1.at[chunk, pl.ds(0, COLS - 1)], recv_row1.at[chunk]).wait()
        rows = []
        for q in range(COLS):
            left = rows0[q, pl.ds(chunk * CHUNK_J, CHUNK_J)].reshape(CHUNK_J * 8, HALF_TP)
            right = rows1[chunk, q].reshape(CHUNK_J * 8, HALF_TP)
            rows.append(jnp.concatenate([left, right], 1))
        rows = filter_rows(rows, gain_ref, twist_ref, [table_ref[n] for n in range(4)])
        for q in range(COLS):
            for half in range(2):
                piece = rows[q][:, half * HALF_TP : (half + 1) * HALF_TP]
                ready[half, chunk, q] = piece.reshape(CHUNK_J, 8, HALF_TP)

        @pl.when(chunk >= 2)
        def _():
            send_ready(1, chunk - 2)

        send_ready(0, chunk)
        return carry

    lax.fori_loop(0, CHUNKS, filter_chunk, 0)
    for chunk in range(CHUNKS - 2, CHUNKS):
        send_ready(1, chunk)

    for half in range(2):
        source = filtered[half]
        for chunk in range(CHUNKS):
            own_ready(half, chunk).wait()
        bytes_of(source.at[pl.ds(0, NJ - GROUP_J)], recv_out.at[half]).wait()
        pltpu.make_async_copy(
            source, filtered_ref.at[:, :, pl.ds(half * HALF_TP, HALF_TP)], out_sem.at[half]
        ).start()

        def pick(step):
            for n in range(4):
                column = here.target(step, n)
                for part in range(TILES):
                    block = column * TILES + part
                    for k in range(2):
                        picked[half, block, k] = source[list_smem[column_me, k, block]]

        def send_picked(column, part):
            remote(
                picked.at[half, column * TILES + part],
                returned.at[half, column_me, part_me],
                send_pick,
                recv_pick.at[half, column_me],
                column,
                part,
            )

        def pick_step(step, carry):
            pick(step)
            for n in range(4):
                each_other(step - 1, n, send_picked)
            return carry

        pick(0)
        lax.fori_loop(1, STEPS, pick_step, 0)
        for n in range(4):
            each_other(STEPS - 1, n, send_picked)
        own = pltpu.make_async_copy(
            picked.at[half, me], returned.at[half, column_me, part_me], own_pick.at[half]
        )
        own.start()
        own.wait()

    def read(step, carry):
        columns = [here.source(step, n) for n in range(4)]
        for column in columns:
            for half in range(2):

                @pl.when(column != column_me)
                def _():
                    bytes_of(returned.at[half, column], recv_pick.at[half, column]).wait()

                @pl.when(column == column_me)
                def _():
                    bytes_of(
                        returned.at[half, column, pl.ds(0, TILES - 1)], recv_pick.at[half, column]
                    ).wait()

        for column in columns:
            for k in range(2):
                slot = 2 * column + k
                row = pl.ds(slot, 1)
                sides = [returned[half, column, :, k].reshape(TR, HALF_TP) for half in range(2)]
                gradient_ref[row, :] = read_tile(
                    jnp.concatenate(sides, 1),
                    ct_ref[slot],
                    pt_ref[slot],
                    cs_ref[row, :],
                    ps_ref[row, :],
                )
        return carry

    lax.fori_loop(0, STEPS, read, 0)
    bytes_of(stage.at[:, pl.ds(0, others)], send_tile).wait()
    bytes_of(owned.at[:, pl.ds(0, NJ - GROUP_J)], send_row).wait()
    bytes_of(ready.at[:, :, pl.ds(0, COLS - 1)], send_out).wait()
    bytes_of(picked.at[:, pl.ds(0, others)], send_pick).wait()
    for half in range(2):
        pltpu.make_async_copy(
            filtered[half],
            filtered_ref.at[:, :, pl.ds(half * HALF_TP, HALF_TP)],
            out_sem.at[half],
        ).wait()


def per_device(values, cycle_taps, phi_taps, cycle_start, phi_start, tile_list, response):
    lists = jnp.transpose(tile_list, (1, 2, 0))
    twist, tables = filter_tables()
    vmem = pl.BlockSpec(memory_space=pltpu.VMEM)
    tile = (8, HALF_TP)
    dma = pltpu.SemaphoreType.DMA
    filtered, gradient = pl.pallas_call(
        whole_kernel,
        in_specs=[pl.BlockSpec(memory_space=pltpu.SMEM)] + [vmem] * 9,
        out_specs=(pl.BlockSpec(memory_space=pl.ANY), vmem),
        out_shape=(
            jax.ShapeDtypeStruct((NJ, 8, TP), F32),
            jax.ShapeDtypeStruct((SLOTS_DEV, PPS), F32),
        ),
        scratch_shapes=[
            pltpu.VMEM((8, HALF_TP), jnp.int32),
            pltpu.SMEM((8, HALF_TP), jnp.int32),
            pltpu.VMEM((HALF, TP), F32),
            pltpu.VMEM((2, COLS * TILES, 2) + tile, F32),
            pltpu.VMEM((NJ + 2,) + tile, F32),
            pltpu.VMEM((NJ + 2,) + tile, F32),
            pltpu.VMEM((2, NJ) + tile, F32),
            pltpu.VMEM((COLS, GROUP_J) + tile, F32),
            pltpu.VMEM((CHUNKS, COLS, CHUNK_J) + tile, F32),
            pltpu.VMEM((2, CHUNKS, COLS, CHUNK_J) + tile, F32),
            pltpu.VMEM((NJ,) + tile, F32),
            pltpu.VMEM((NJ,) + tile, F32),
            pltpu.VMEM((2, COLS * TILES, 2) + tile, F32),
            pltpu.VMEM((2, COLS, TILES, 2) + tile, F32),
            dma,
            dma((2,)),
            dma,
            dma((2,)),
            dma((2,)),
            dma,
            dma,
            dma((CHUNKS,)),
            dma((1 + CHUNKS,)),
            dma,
            dma((2,)),
            dma((2, CHUNKS)),
            dma,
            dma((2, COLS)),
            dma((2,)),
        ],
        compiler_params=pltpu.CompilerParams(
            collective_id=0, has_side_effects=True, vmem_limit_bytes=56 << 20
        ),
        name="whole",
    )(
        lists,
        lists,
        values[0],
        cycle_taps[0],
        phi_taps[0],
        cycle_start[0],
        phi_start[0],
        response,
        jnp.asarray(twist),
        jnp.asarray(tables),
    )
    return filtered, gradient[None]


def solution(mesh):
    return jax.shard_map(
        per_device,
        mesh=mesh,
        in_specs=(
            P(("pts", "tile"), None, None),
            P(("pts", "tile"), None, None, None),
            P(("pts", "tile"), None, None, None),
            P(("pts", "tile"), None, None),
            P(("pts", "tile"), None, None),
            P(),
            P(),
        ),
        out_specs=(P(None, "tile", "pts"), P(("pts", "tile"), None, None)),
        check_vma=False,
    )
```

```python
import functools
import math

import jax
import jax.numpy as jnp
import numpy as np
from jax import lax
from jax.experimental import pallas as pl
from jax.experimental.pallas import tpu as pltpu
from jax.sharding import PartitionSpec as P

NPHI = 8192
TR = 32
NJ = 256
TP = 256
PPS = 1024
COLS = 32
SLOTS_DEV = 64
HALF = COLS // 2 + 1
HALF_TP = TP // 2

F32 = jnp.float32
BF16 = jnp.bfloat16
CONTRACT_LAST = (((1,), (1,)), ((), ()))


def split(x):
    high = x.astype(BF16)
    return high, (x - high.astype(F32)).astype(BF16)


def place(taps, start):
    count = taps.shape[1]
    row = lax.broadcasted_iota(jnp.int32, (8, count), 0)
    starts = jnp.broadcast_to(start, (8, count))
    for bit in (1, 2, 4):
        taps = jnp.where((starts & bit) != 0, pltpu.roll(taps, bit, 0), taps)
    return taps, (starts - row + 7) >> 3


def expand(parts, group, groups, first=0):
    group = group.astype(F32)
    count = group.shape[1]
    pair = jnp.concatenate([group, group - 1.0], 0).astype(BF16)
    doubled = [jnp.concatenate([part.astype(F32)] * 2, 0).astype(BF16) for part in parts]
    zero = jnp.zeros((16, count), BF16)
    rows = [[] for _ in parts]
    for index in range(groups // 2):
        mask = pair == jnp.asarray(2 * index + first, BF16)
        for out, part in zip(rows, doubled):
            out.append(jnp.where(mask, part, zero))
    return [jnp.concatenate(out, 0) for out in rows]


MESH = pl.DeviceIdType.MESH
TILES = 4
FAR_FIRST = (2, 1, 3, 0)
STEPS = COLS // 4
SELF_STEP = 5


def spread_tile(half, values, cycle_taps, phi_taps, cycle_start, phi_start):
    cycle, cycle_group = place(cycle_taps * values, cycle_start)
    phi, phi_group = place(phi_taps, phi_start)
    cycle_high, cycle_low = expand(split(cycle), cycle_group, TR // 8)
    phi_high, phi_low = expand(split(phi), phi_group, HALF_TP // 8, half * (HALF_TP // 8))
    stacked = jnp.concatenate([cycle_high, cycle_low], 0)
    first = lax.dot_general(phi_high, stacked, CONTRACT_LAST, preferred_element_type=F32)
    second = lax.dot_general(phi_low, cycle_high, CONTRACT_LAST, preferred_element_type=F32)
    return (first[:, :TR] + first[:, TR:] + second).T


def read_tile(tile, cycle_taps, phi_taps, cycle_start, phi_start):
    tile_high, tile_low = split(tile)
    cycle, cycle_group = place(cycle_taps, cycle_start)
    phi, phi_group = place(phi_taps, phi_start)
    cycle_high, cycle_low = expand(split(cycle), cycle_group, TR // 8)
    right = jnp.concatenate([cycle_high, cycle_low, cycle_high], 0)
    left = jnp.concatenate([tile_high, tile_high, tile_low], 0).T
    along = jnp.dot(left, right, preferred_element_type=F32)
    picked = jnp.zeros((8, PPS), F32)
    for g in range(TP // 8):
        picked = jnp.where(phi_group == g, along[8 * g : 8 * g + 8], picked)
    return jnp.sum(picked * phi, 0, keepdims=True)


class Place:
    def __init__(self):
        self.column = lax.axis_index("pts")
        self.part = lax.axis_index("tile")
        z, self.y = self.column // 8, lax.rem(self.column // 2, 4)
        self.core = lax.rem(self.column, 2)
        self.ahead = [lax.rem(z + dz, 4) * 8 for dz in FAR_FIRST]
        self.behind = [lax.rem(z + 4 - dz, 4) * 8 for dz in FAR_FIRST]
        self.parts = [lax.rem(self.part + dx, 4) for dx in FAR_FIRST]

    def core_at(self, step):
        return lax.rem(self.core + 1 + step // 4, 2)

    def target(self, step, n):
        return self.ahead[n] + 2 * lax.rem(self.y + step + n, 4) + self.core_at(step)

    def source(self, step, n):
        return self.behind[n] + 2 * lax.rem(self.y + 16 - step - n, 4) + self.core_at(step)


def unless_self(step, n, action):
    if n != 3:
        action()
    elif isinstance(step, int):
        if step != SELF_STEP:
            action()
    else:
        pl.when(step != SELF_STEP)(action)


def greet(here):
    barrier = pltpu.get_barrier_semaphore()
    for step in range(STEPS):
        for n in range(4):
            column = here.target(step, n)
            for dx, part in zip(FAR_FIRST, here.parts):
                if (step, n, dx) != (SELF_STEP, 3, 0):
                    pl.semaphore_signal(
                        barrier, inc=1, device_id=(column, part), device_id_type=MESH
                    )
    return barrier


def bytes_of(ref, sem):
    return pltpu.make_async_copy(ref, ref, sem)


def times(re, im, cos, sin):
    return re * cos - im * sin, re * sin + im * cos


def turn(re, im, angle):
    cos, sin = math.cos(angle), math.sin(angle)
    if abs(sin) < 1e-12:
        return (re, im) if cos > 0 else (-re, -im)
    if abs(cos) < 1e-12:
        return (-im, re) if sin > 0 else (im, -re)
    return re * cos - im * sin, re * sin + im * cos


def real_fft(x):
    n = len(x)
    if n == 1:
        return [(x[0], None)]
    if n == 2:
        return [(x[0] + x[1], None), (x[0] - x[1], None)]
    even, odd = real_fft(x[0::2]), real_fft(x[1::2])
    out = [None] * (n // 2 + 1)
    out[0] = (even[0][0] + odd[0][0], None)
    out[n // 2] = (even[0][0] - odd[0][0], None)
    for k in range(1, n // 4):
        er, ei = even[k]
        tr, ti = turn(odd[k][0], odd[k][1], -2.0 * math.pi * k / n)
        out[k] = (er + tr, ei + ti)
        out[n // 2 - k] = (er - tr, ti - ei)
    quarter = n // 4
    out[quarter] = (even[quarter][0], -odd[quarter][0])
    return out


def real_inverse(spec):
    half = len(spec) - 1
    n = 2 * half
    if n == 2:
        return [spec[0][0] + spec[1][0], spec[0][0] - spec[1][0]]
    even, odd = [None] * (half // 2 + 1), [None] * (half // 2 + 1)
    even[0] = (spec[0][0] + spec[half][0], None)
    odd[0] = (spec[0][0] - spec[half][0], None)
    for k in range(1, half // 2):
        ar, ai = spec[k]
        br, bi = spec[half - k]
        even[k] = (ar + br, ai - bi)
        odd[k] = turn(ar - br, ai + bi, 2.0 * math.pi * k / n)
    middle = half // 2
    even[middle] = (2.0 * spec[middle][0], None)
    odd[middle] = (-2.0 * spec[middle][1], None)
    out = [None] * n
    out[0::2] = real_inverse(even)
    out[1::2] = real_inverse(odd)
    return out


def times_table(rows, table_high, table_low):
    high, low = split(rows)
    dot = functools.partial(jnp.dot, preferred_element_type=F32)
    return dot(high, table_high) + dot(high, table_low) + dot(low, table_high)


def filter_rows(rows, gain_ref, twist_ref, tables):
    cycles = rows[0].shape[0]
    spec = real_fft(rows)
    reals, imags = [], []
    for k in range(HALF):
        cos, sin = twist_ref[0, k : k + 1, :], twist_ref[1, k : k + 1, :]
        re, im = spec[k]
        if im is None:
            reals.append(re * cos)
            imags.append(-re * sin)
        else:
            re, im = times(re, im, cos, -sin)
            reals.append(re)
            imags.append(im)
    count = HALF * cycles
    both = times_table(jnp.concatenate(reals + imags, 0), tables[0], tables[1])
    first, last = both[:count], both[count:]
    freq_re = first[:, :TP] + last[:, TP:]
    freq_im = last[:, :TP] - first[:, TP:]
    gains = [jnp.broadcast_to(gain_ref[k : k + 1, :], (cycles, TP)) for k in range(HALF)]
    gain = jnp.concatenate(gains, 0)
    both = times_table(
        jnp.concatenate([freq_re * gain, freq_im * gain], 0), tables[2], tables[3]
    )
    first, last = both[:count], both[count:]
    back_re = first[:, :TP] - last[:, TP:]
    back_im = last[:, :TP] + first[:, TP:]
    spec = []
    for k in range(HALF):
        cos, sin = twist_ref[0, k : k + 1, :], twist_ref[1, k : k + 1, :]
        re, im = back_re[k * cycles : (k + 1) * cycles], back_im[k * cycles : (k + 1) * cycles]
        spec.append(times(re, im, cos, sin))
    return real_inverse(spec)


def filter_tables():
    index = np.arange(TP)
    low_half = 4 * (np.arange(HALF_TP) % COLS) + np.arange(HALF_TP) // COLS
    order = np.concatenate([low_half, TP - 1 - low_half])
    angle = 2.0 * np.pi * (np.outer(index, order) % TP) / TP
    tables = []
    for cos, sin in [(np.cos(angle), np.sin(angle)), (np.cos(angle).T, np.sin(angle).T)]:
        table = np.concatenate([cos, sin], 1).astype(np.float32)
        high = table.astype(BF16)
        tables += [high, (table - high.astype(np.float32)).astype(BF16)]
    angle = 2.0 * np.pi * np.outer(np.arange(HALF), index) / NPHI
    return np.stack([np.cos(angle), np.sin(angle)]).astype(np.float32), np.stack(tables)


def gain_table(response_ref):
    rows = [response_ref[HALF_TP * s : HALF_TP * (s + 1)].reshape(1, HALF_TP) for s in range(COLS)]
    turned = jnp.concatenate(rows, 0).T
    grid = jnp.concatenate([turned[COLS * b : COLS * (b + 1)] for b in range(4)], 1)
    lane = lax.broadcasted_iota(jnp.int32, (8, HALF_TP), 1)
    zeroth = jnp.broadcast_to(grid[:1], (8, HALF_TP))
    ahead = jnp.where(
        lane < 3 * COLS, pltpu.roll(zeroth, 3 * COLS, 1), pltpu.roll(zeroth, 3 * COLS - 1, 1)
    )
    last = response_ref[NPHI // 2 : NPHI // 2 + 1].reshape(1, 1)
    ahead = jnp.where(lane == HALF_TP - 1, jnp.broadcast_to(last, (8, HALF_TP)), ahead)
    mirrored = [ahead[:1]] + [grid[COLS - k : COLS - k + 1] for k in range(1, HALF)]
    both = jnp.concatenate([grid[:HALF], jnp.concatenate(mirrored, 0)], 1)
    return both * (1.0 / NPHI)


def same_block_links(wanted):
    lane = lax.broadcasted_iota(jnp.int32, (HALF_TP, HALF_TP), 1)
    across = [jnp.broadcast_to(wanted[k : k + 1], (HALF_TP, HALF_TP)) for k in range(2)]
    down = [x.T for x in across]
    item = [2 * lax.broadcasted_iota(jnp.int32, (HALF_TP, HALF_TP), 0) + k for k in range(2)]

    def latest(matches):
        found = [
            jnp.max(jnp.where(match, item[k], -1), 0, keepdims=True)
            for k, match in enumerate(matches)
        ]
        found = jnp.maximum(found[0], found[1])
        return jnp.where(found < 0, NJ, found)

    links = []
    for k in range(2):
        here = 2 * lane + k
        links.append(
            latest([jnp.logical_and(down[n] == across[k], item[n] < here) for n in range(2)])
        )
    for half in range(2):
        links.append(latest([down[n] == lane + HALF_TP * half for n in range(2)]))
    return links


def within(entry):
    return jnp.minimum(jnp.maximum(entry, 0), NJ)


CHUNKS = 4
CHUNK_J = 2
GROUP_J = CHUNKS * CHUNK_J


def whole_kernel(
    list_smem, list_vmem, v_hbm, ct_hbm, pt_hbm, cs_hbm, ps_hbm,
    response_hbm, twist_hbm, table_hbm,
    filtered_ref, gradient_ref,
    v_ref, ct_ref, pt_ref, cs_ref, ps_ref, response_ref, twist_ref, table_ref,
    links_vmem, links, gain_ref, stage, arrived0, arrived1, owned, rows0, rows1,
    ready, filtered0, filtered1, picked, returned,
    load_sem, links_sem, out_sem, send_tile, recv_tile, own_tile,
    send_row, recv_row0, recv_row1, own_row, send_out, recv_out, own_out,
    send_pick, recv_pick, own_pick,
):
    loads = [
        pltpu.make_async_copy(source, target, load_sem.at[n])
        for n, (source, target) in enumerate(
            [
                (cs_hbm, cs_ref),
                (ps_hbm, ps_ref),
                (v_hbm, v_ref),
                (ct_hbm, ct_ref),
                (pt_hbm, pt_ref),
                (response_hbm, response_ref),
                (twist_hbm, twist_ref),
                (table_hbm, table_ref),
            ]
        )
    ]
    for load in loads:
        load.start()
    here = Place()
    barrier = greet(here)
    column_me, part_me = here.column, here.part
    me = column_me * TILES + part_me
    arrived, filtered = (arrived0, arrived1), (filtered0, filtered1)
    others = COLS * TILES - 1

    def each_other(step, n, action):
        column = here.target(step, n)
        for dx, part in zip(FAR_FIRST, here.parts):
            send = functools.partial(action, column, part)
            if dx:
                send()
            else:
                unless_self(step, n, send)

    def each_column(action):
        def visit(step, carry):
            for n in range(4):
                unless_self(step, n, functools.partial(action, here.target(step, n)))
            return carry

        lax.fori_loop(0, STEPS, visit, 0)

    def remote(source, target, sent, received, column, part):
        pltpu.make_async_remote_copy(
            source, target, sent, received, device_id=(column, part), device_id_type=MESH
        ).start()

    for n, link in enumerate(same_block_links(list_vmem[column_me])):
        links_vmem[n : n + 1, :] = link
    for load in loads[:6]:
        load.wait()
    gain_ref[...] = gain_table(response_ref)
    for half in range(2):
        arrived[half][NJ] = jnp.zeros((8, HALF_TP), F32)

    def compute(half, step):
        for n in range(4):
            column = here.target(step, n)
            for k in range(2):
                slot = 2 * column + k
                row = pl.ds(slot, 1)
                tile = spread_tile(
                    half, v_ref[row, :], ct_ref[slot], pt_ref[slot], cs_ref[row, :], ps_ref[row, :]
                )
                stage[half, pl.ds(column * TILES, TILES), k] = tile.reshape(TILES, 8, HALF_TP)

    def dispatch(half, step):
        def send(column, part):
            remote(
                stage.at[half, column * TILES + part],
                arrived[half].at[pl.ds(2 * me, 2)],
                send_tile,
                recv_tile.at[half],
                column,
                part,
            )

        for n in range(4):
            each_other(step, n, send)

    def own_tiles(half):
        return pltpu.make_async_copy(
            stage.at[half, me], arrived[half].at[pl.ds(2 * me, 2)], own_tile.at[half]
        )

    copy_links = pltpu.make_async_copy(links_vmem, links, links_sem)
    compute(0, 0)
    copy_links.start()
    pl.semaphore_wait(barrier, others)
    for half in range(2):

        def spread_step(step, carry):
            compute(half, step)
            dispatch(half, step - 1)
            return carry

        if half:
            compute(half, 0)
            dispatch(0, STEPS - 1)
            own_tiles(0).start()
        lax.fori_loop(1, STEPS, spread_step, 0)
    dispatch(1, STEPS - 1)
    own_tiles(1).start()
    copy_links.wait()

    for half in range(2):
        tiles = arrived[half]
        bytes_of(tiles.at[pl.ds(0, 2 * others)], recv_tile.at[half]).wait()
        own_tiles(half).wait()

        def add(b, carry):
            for k in range(2):
                tiles[2 * b + k] = tiles[2 * b + k] + tiles[within(links[k, b])]
            return carry

        lax.fori_loop(0, COLS * TILES, add, 0, unroll=4)

        def gather(column):
            first = column // 16
            for j in range(GROUP_J):
                entry = links[2 + first, (column - 16 * first) * GROUP_J + j]
                owned[half, column * GROUP_J + j] = tiles[within(entry)]

        if half == 0:

            def send_rows(column):
                remote(
                    owned.at[0, pl.ds(column * GROUP_J, GROUP_J)],
                    rows0.at[column_me],
                    send_row,
                    recv_row0,
                    column,
                    part_me,
                )

            def row_step(step, carry):
                for n in range(4):
                    gather(here.target(step, n))
                for n in range(4):
                    column = here.target(step - 1, n)
                    unless_self(step - 1, n, functools.partial(send_rows, column))
                return carry

            for n in range(4):
                gather(here.target(0, n))
            lax.fori_loop(1, STEPS, row_step, 0)
            for n in range(4):
                send_rows(here.target(STEPS - 1, n))
        else:

            def row_step(step, carry):
                for n in range(4):
                    gather(here.target(step, n))
                return carry

            lax.fori_loop(0, STEPS, row_step, 0)

            def send_chunk(chunk, carry):
                def send(column):
                    remote(
                        owned.at[1, pl.ds(column * GROUP_J + chunk * CHUNK_J, CHUNK_J)],
                        rows1.at[chunk, column_me],
                        send_row,
                        recv_row1.at[chunk],
                        column,
                        part_me,
                    )

                each_column(send)
                return carry

            lax.fori_loop(0, CHUNKS, send_chunk, 0)

    own_rows = [
        pltpu.make_async_copy(
            owned.at[0, pl.ds(column_me * GROUP_J, GROUP_J)], rows0.at[column_me], own_row.at[0]
        )
    ]
    for chunk in range(CHUNKS):
        own_rows.append(
            pltpu.make_async_copy(
                owned.at[1, pl.ds(column_me * GROUP_J + chunk * CHUNK_J, CHUNK_J)],
                rows1.at[chunk, column_me],
                own_row.at[1 + chunk],
            )
        )
    for copy in own_rows:
        copy.start()
    for copy in own_rows:
        copy.wait()
    bytes_of(rows0.at[pl.ds(0, COLS - 1)], recv_row0).wait()
    for load in loads[6:]:
        load.wait()

    def chunk_rows(chunk):
        return pl.ds(column_me * GROUP_J + chunk * CHUNK_J, CHUNK_J)

    def own_ready(half, chunk):
        return pltpu.make_async_copy(
            ready.at[half, chunk, column_me],
            filtered[half].at[chunk_rows(chunk)],
            own_out.at[half, chunk],
        )

    def send_ready(half, chunk):
        def send(column):
            remote(
                ready.at[half, chunk, column],
                filtered[half].at[chunk_rows(chunk)],
                send_out,
                recv_out.at[half],
                column,
                part_me,
            )

        each_column(send)
        own_ready(half, chunk).start()

    def filter_chunk(chunk, carry):
        bytes_of(rows1.at[chunk, pl.ds(0, COLS - 1)], recv_row1.at[chunk]).wait()
        rows = []
        for q in range(COLS):
            left = rows0[q, pl.ds(chunk * CHUNK_J, CHUNK_J)].reshape(CHUNK_J * 8, HALF_TP)
            right = rows1[chunk, q].reshape(CHUNK_J * 8, HALF_TP)
            rows.append(jnp.concatenate([left, right], 1))
        rows = filter_rows(rows, gain_ref, twist_ref, [table_ref[n] for n in range(4)])
        for q in range(COLS):
            for half in range(2):
                piece = rows[q][:, half * HALF_TP : (half + 1) * HALF_TP]
                ready[half, chunk, q] = piece.reshape(CHUNK_J, 8, HALF_TP)

        @pl.when(chunk >= 2)
        def _():
            send_ready(1, chunk - 2)

        send_ready(0, chunk)
        return carry

    lax.fori_loop(0, CHUNKS, filter_chunk, 0)
    for chunk in range(CHUNKS - 2, CHUNKS):
        send_ready(1, chunk)

    for half in range(2):
        source = filtered[half]
        for chunk in range(CHUNKS):
            own_ready(half, chunk).wait()
        bytes_of(source.at[pl.ds(0, NJ - GROUP_J)], recv_out.at[half]).wait()
        pltpu.make_async_copy(
            source, filtered_ref.at[:, :, pl.ds(half * HALF_TP, HALF_TP)], out_sem.at[half]
        ).start()

        def pick(step):
            for n in range(4):
                column = here.target(step, n)
                for part in range(TILES):
                    block = column * TILES + part
                    for k in range(2):
                        picked[half, block, k] = source[list_smem[column_me, k, block]]

        def send_picked(column, part):
            remote(
                picked.at[half, column * TILES + part],
                returned.at[half, column_me, part_me],
                send_pick,
                recv_pick.at[half, column_me],
                column,
                part,
            )

        def pick_step(step, carry):
            pick(step)
            for n in range(4):
                each_other(step - 1, n, send_picked)
            return carry

        pick(0)
        lax.fori_loop(1, STEPS, pick_step, 0)
        for n in range(4):
            each_other(STEPS - 1, n, send_picked)
        own = pltpu.make_async_copy(
            picked.at[half, me], returned.at[half, column_me, part_me], own_pick.at[half]
        )
        own.start()
        own.wait()

    def read(step, carry):
        columns = [here.source(step, n) for n in range(4)]
        for column in columns:
            for half in range(2):

                @pl.when(column != column_me)
                def _():
                    bytes_of(returned.at[half, column], recv_pick.at[half, column]).wait()

                @pl.when(column == column_me)
                def _():
                    bytes_of(
                        returned.at[half, column, pl.ds(0, TILES - 1)], recv_pick.at[half, column]
                    ).wait()

        for column in columns:
            for k in range(2):
                slot = 2 * column + k
                row = pl.ds(slot, 1)
                sides = [returned[half, column, :, k].reshape(TR, HALF_TP) for half in range(2)]
                gradient_ref[row, :] = read_tile(
                    jnp.concatenate(sides, 1),
                    ct_ref[slot],
                    pt_ref[slot],
                    cs_ref[row, :],
                    ps_ref[row, :],
                )
        return carry

    lax.fori_loop(0, STEPS, read, 0)
    bytes_of(stage.at[:, pl.ds(0, others)], send_tile).wait()
    bytes_of(owned.at[:, pl.ds(0, NJ - GROUP_J)], send_row).wait()
    bytes_of(ready.at[:, :, pl.ds(0, COLS - 1)], send_out).wait()
    bytes_of(picked.at[:, pl.ds(0, others)], send_pick).wait()
    for half in range(2):
        pltpu.make_async_copy(
            filtered[half],
            filtered_ref.at[:, :, pl.ds(half * HALF_TP, HALF_TP)],
            out_sem.at[half],
        ).wait()


def per_device(values, cycle_taps, phi_taps, cycle_start, phi_start, tile_list, response):
    lists = jnp.transpose(tile_list, (1, 2, 0))
    twist, tables = filter_tables()
    vmem = pl.BlockSpec(memory_space=pltpu.VMEM)
    hbm = pl.BlockSpec(memory_space=pltpu.HBM)
    tile = (8, HALF_TP)
    dma = pltpu.SemaphoreType.DMA
    filtered, gradient = pl.pallas_call(
        whole_kernel,
        in_specs=[pl.BlockSpec(memory_space=pltpu.SMEM), vmem] + [hbm] * 8,
        out_specs=(pl.BlockSpec(memory_space=pl.ANY), vmem),
        out_shape=(
            jax.ShapeDtypeStruct((NJ, 8, TP), F32),
            jax.ShapeDtypeStruct((SLOTS_DEV, PPS), F32),
        ),
        scratch_shapes=[
            pltpu.VMEM(values.shape[1:], F32),
            pltpu.VMEM(cycle_taps.shape[1:], F32),
            pltpu.VMEM(phi_taps.shape[1:], F32),
            pltpu.VMEM(cycle_start.shape[1:], jnp.int32),
            pltpu.VMEM(phi_start.shape[1:], jnp.int32),
            pltpu.VMEM(response.shape, F32),
            pltpu.VMEM(twist.shape, F32),
            pltpu.VMEM(tables.shape, BF16),
            pltpu.VMEM((8, HALF_TP), jnp.int32),
            pltpu.SMEM((8, HALF_TP), jnp.int32),
            pltpu.VMEM((HALF, TP), F32),
            pltpu.VMEM((2, COLS * TILES, 2) + tile, F32),
            pltpu.VMEM((NJ + 2,) + tile, F32),
            pltpu.VMEM((NJ + 2,) + tile, F32),
            pltpu.VMEM((2, NJ) + tile, F32),
            pltpu.VMEM((COLS, GROUP_J) + tile, F32),
            pltpu.VMEM((CHUNKS, COLS, CHUNK_J) + tile, F32),
            pltpu.VMEM((2, CHUNKS, COLS, CHUNK_J) + tile, F32),
            pltpu.VMEM((NJ,) + tile, F32),
            pltpu.VMEM((NJ,) + tile, F32),
            pltpu.VMEM((2, COLS * TILES, 2) + tile, F32),
            pltpu.VMEM((2, COLS, TILES, 2) + tile, F32),
            dma((8,)),
            dma,
            dma((2,)),
            dma,
            dma((2,)),
            dma((2,)),
            dma,
            dma,
            dma((CHUNKS,)),
            dma((1 + CHUNKS,)),
            dma,
            dma((2,)),
            dma((2, CHUNKS)),
            dma,
            dma((2, COLS)),
            dma((2,)),
        ],
        compiler_params=pltpu.CompilerParams(
            collective_id=0, has_side_effects=True, vmem_limit_bytes=57 << 20
        ),
        name="whole",
    )(
        lists,
        lists,
        values[0],
        cycle_taps[0],
        phi_taps[0],
        cycle_start[0],
        phi_start[0],
        response,
        jnp.asarray(twist),
        jnp.asarray(tables),
    )
    return filtered, gradient[None]


def solution(mesh):
    return jax.shard_map(
        per_device,
        mesh=mesh,
        in_specs=(
            P(("pts", "tile"), None, None),
            P(("pts", "tile"), None, None, None),
            P(("pts", "tile"), None, None, None),
            P(("pts", "tile"), None, None),
            P(("pts", "tile"), None, None),
            P(),
            P(),
        ),
        out_specs=(P(None, "tile", "pts"), P(("pts", "tile"), None, None)),
        check_vma=False,
    )
```

```python
import functools
import math

import jax
import jax.numpy as jnp
import numpy as np
from jax import lax
from jax.experimental import pallas as pl
from jax.experimental.pallas import tpu as pltpu
from jax.sharding import PartitionSpec as P

NPHI = 8192
TR = 32
NJ = 256
TP = 256
PPS = 1024
COLS = 32
SLOTS_DEV = 64
HALF = COLS // 2 + 1
HALF_TP = TP // 2

F32 = jnp.float32
BF16 = jnp.bfloat16
CONTRACT_LAST = (((1,), (1,)), ((), ()))


def split(x):
    high = x.astype(BF16)
    return high, (x - high.astype(F32)).astype(BF16)


def place(taps, start):
    count = taps.shape[1]
    row = lax.broadcasted_iota(jnp.int32, (8, count), 0)
    starts = jnp.broadcast_to(start, (8, count))
    for bit in (1, 2, 4):
        taps = jnp.where((starts & bit) != 0, pltpu.roll(taps, bit, 0), taps)
    return taps, (starts - row + 7) >> 3


def expand(parts, group, groups, first=0):
    group = group.astype(F32)
    count = group.shape[1]
    pair = jnp.concatenate([group, group - 1.0], 0).astype(BF16)
    doubled = [jnp.concatenate([part.astype(F32)] * 2, 0).astype(BF16) for part in parts]
    zero = jnp.zeros((16, count), BF16)
    rows = [[] for _ in parts]
    for index in range(groups // 2):
        mask = pair == jnp.asarray(2 * index + first, BF16)
        for out, part in zip(rows, doubled):
            out.append(jnp.where(mask, part, zero))
    return [jnp.concatenate(out, 0) for out in rows]


MESH = pl.DeviceIdType.MESH
TILES = 4
FAR_FIRST = (2, 1, 3, 0)
STEPS = COLS // 4
SELF_STEP = 5


def spread_tile(half, values, cycle_taps, phi_taps, cycle_start, phi_start):
    cycle, cycle_group = place(cycle_taps * values, cycle_start)
    phi, phi_group = place(phi_taps, phi_start)
    cycle_high, cycle_low = expand(split(cycle), cycle_group, TR // 8)
    phi_high, phi_low = expand(split(phi), phi_group, HALF_TP // 8, half * (HALF_TP // 8))
    stacked = jnp.concatenate([cycle_high, cycle_low], 0)
    first = lax.dot_general(phi_high, stacked, CONTRACT_LAST, preferred_element_type=F32)
    second = lax.dot_general(phi_low, cycle_high, CONTRACT_LAST, preferred_element_type=F32)
    return (first[:, :TR] + first[:, TR:] + second).T


def read_tile(tile, cycle_taps, phi_taps, cycle_start, phi_start):
    tile_high, tile_low = split(tile)
    cycle, cycle_group = place(cycle_taps, cycle_start)
    phi, phi_group = place(phi_taps, phi_start)
    cycle_high, cycle_low = expand(split(cycle), cycle_group, TR // 8)
    right = jnp.concatenate([cycle_high, cycle_low, cycle_high], 0)
    left = jnp.concatenate([tile_high, tile_high, tile_low], 0).T
    along = jnp.dot(left, right, preferred_element_type=F32)
    picked = jnp.zeros((8, PPS), F32)
    for g in range(TP // 8):
        picked = jnp.where(phi_group == g, along[8 * g : 8 * g + 8], picked)
    return jnp.sum(picked * phi, 0, keepdims=True)


class Place:
    def __init__(self):
        self.column = lax.axis_index("pts")
        self.part = lax.axis_index("tile")
        z, self.y = self.column // 8, lax.rem(self.column // 2, 4)
        self.core = lax.rem(self.column, 2)
        self.ahead = [lax.rem(z + dz, 4) * 8 for dz in FAR_FIRST]
        self.behind = [lax.rem(z + 4 - dz, 4) * 8 for dz in FAR_FIRST]
        self.parts = [lax.rem(self.part + dx, 4) for dx in FAR_FIRST]

    def core_at(self, step):
        return lax.rem(self.core + 1 + step // 4, 2)

    def target(self, step, n):
        return self.ahead[n] + 2 * lax.rem(self.y + step + n, 4) + self.core_at(step)

    def source(self, step, n):
        return self.behind[n] + 2 * lax.rem(self.y + 16 - step - n, 4) + self.core_at(step)


def unless_self(step, n, action):
    if n != 3:
        action()
    elif isinstance(step, int):
        if step != SELF_STEP:
            action()
    else:
        pl.when(step != SELF_STEP)(action)


def greet(here):
    barrier = pltpu.get_barrier_semaphore()
    for step in range(STEPS):
        for n in range(4):
            column = here.target(step, n)
            for dx, part in zip(FAR_FIRST, here.parts):
                if (step, n, dx) != (SELF_STEP, 3, 0):
                    pl.semaphore_signal(
                        barrier, inc=1, device_id=(column, part), device_id_type=MESH
                    )
    return barrier


def bytes_of(ref, sem):
    return pltpu.make_async_copy(ref, ref, sem)


def times(re, im, cos, sin):
    return re * cos - im * sin, re * sin + im * cos


def turn(re, im, angle):
    cos, sin = math.cos(angle), math.sin(angle)
    if abs(sin) < 1e-12:
        return (re, im) if cos > 0 else (-re, -im)
    if abs(cos) < 1e-12:
        return (-im, re) if sin > 0 else (im, -re)
    return re * cos - im * sin, re * sin + im * cos


def real_fft(x):
    n = len(x)
    if n == 1:
        return [(x[0], None)]
    if n == 2:
        return [(x[0] + x[1], None), (x[0] - x[1], None)]
    even, odd = real_fft(x[0::2]), real_fft(x[1::2])
    out = [None] * (n // 2 + 1)
    out[0] = (even[0][0] + odd[0][0], None)
    out[n // 2] = (even[0][0] - odd[0][0], None)
    for k in range(1, n // 4):
        er, ei = even[k]
        tr, ti = turn(odd[k][0], odd[k][1], -2.0 * math.pi * k / n)
        out[k] = (er + tr, ei + ti)
        out[n // 2 - k] = (er - tr, ti - ei)
    quarter = n // 4
    out[quarter] = (even[quarter][0], -odd[quarter][0])
    return out


def real_inverse(spec):
    half = len(spec) - 1
    n = 2 * half
    if n == 2:
        return [spec[0][0] + spec[1][0], spec[0][0] - spec[1][0]]
    even, odd = [None] * (half // 2 + 1), [None] * (half // 2 + 1)
    even[0] = (spec[0][0] + spec[half][0], None)
    odd[0] = (spec[0][0] - spec[half][0], None)
    for k in range(1, half // 2):
        ar, ai = spec[k]
        br, bi = spec[half - k]
        even[k] = (ar + br, ai - bi)
        odd[k] = turn(ar - br, ai + bi, 2.0 * math.pi * k / n)
    middle = half // 2
    even[middle] = (2.0 * spec[middle][0], None)
    odd[middle] = (-2.0 * spec[middle][1], None)
    out = [None] * n
    out[0::2] = real_inverse(even)
    out[1::2] = real_inverse(odd)
    return out


def times_table(rows, table_high, table_low):
    high, low = split(rows)
    dot = functools.partial(jnp.dot, preferred_element_type=F32)
    return dot(high, table_high) + dot(high, table_low) + dot(low, table_high)


def filter_rows(rows, gain_ref, twist_ref, tables):
    cycles = rows[0].shape[0]
    spec = real_fft(rows)
    reals, imags = [], []
    for k in range(HALF):
        cos, sin = twist_ref[0, k : k + 1, :], twist_ref[1, k : k + 1, :]
        re, im = spec[k]
        if im is None:
            reals.append(re * cos)
            imags.append(-re * sin)
        else:
            re, im = times(re, im, cos, -sin)
            reals.append(re)
            imags.append(im)
    count = HALF * cycles
    both = times_table(jnp.concatenate(reals + imags, 0), tables[0], tables[1])
    first, last = both[:count], both[count:]
    freq_re = first[:, :TP] + last[:, TP:]
    freq_im = last[:, :TP] - first[:, TP:]
    gains = [jnp.broadcast_to(gain_ref[k : k + 1, :], (cycles, TP)) for k in range(HALF)]
    gain = jnp.concatenate(gains, 0)
    both = times_table(
        jnp.concatenate([freq_re * gain, freq_im * gain], 0), tables[2], tables[3]
    )
    first, last = both[:count], both[count:]
    back_re = first[:, :TP] - last[:, TP:]
    back_im = last[:, :TP] + first[:, TP:]
    spec = []
    for k in range(HALF):
        cos, sin = twist_ref[0, k : k + 1, :], twist_ref[1, k : k + 1, :]
        re, im = back_re[k * cycles : (k + 1) * cycles], back_im[k * cycles : (k + 1) * cycles]
        spec.append(times(re, im, cos, sin))
    return real_inverse(spec)


def filter_tables():
    index = np.arange(TP)
    low_half = 4 * (np.arange(HALF_TP) % COLS) + np.arange(HALF_TP) // COLS
    order = np.concatenate([low_half, TP - 1 - low_half])
    angle = 2.0 * np.pi * (np.outer(index, order) % TP) / TP
    tables = []
    for cos, sin in [(np.cos(angle), np.sin(angle)), (np.cos(angle).T, np.sin(angle).T)]:
        table = np.concatenate([cos, sin], 1).astype(np.float32)
        high = table.astype(BF16)
        tables += [high, (table - high.astype(np.float32)).astype(BF16)]
    angle = 2.0 * np.pi * np.outer(np.arange(HALF), index) / NPHI
    return np.stack([np.cos(angle), np.sin(angle)]).astype(np.float32), np.stack(tables)


def gain_table(response_ref):
    rows = [response_ref[HALF_TP * s : HALF_TP * (s + 1)].reshape(1, HALF_TP) for s in range(COLS)]
    turned = jnp.concatenate(rows, 0).T
    grid = jnp.concatenate([turned[COLS * b : COLS * (b + 1)] for b in range(4)], 1)
    lane = lax.broadcasted_iota(jnp.int32, (8, HALF_TP), 1)
    zeroth = jnp.broadcast_to(grid[:1], (8, HALF_TP))
    ahead = jnp.where(
        lane < 3 * COLS, pltpu.roll(zeroth, 3 * COLS, 1), pltpu.roll(zeroth, 3 * COLS - 1, 1)
    )
    last = response_ref[NPHI // 2 : NPHI // 2 + 1].reshape(1, 1)
    ahead = jnp.where(lane == HALF_TP - 1, jnp.broadcast_to(last, (8, HALF_TP)), ahead)
    mirrored = [ahead[:1]] + [grid[COLS - k : COLS - k + 1] for k in range(1, HALF)]
    both = jnp.concatenate([grid[:HALF], jnp.concatenate(mirrored, 0)], 1)
    return both * (1.0 / NPHI)


def same_block_links(wanted):
    lane = lax.broadcasted_iota(jnp.int32, (HALF_TP, HALF_TP), 1)
    across = [jnp.broadcast_to(wanted[k : k + 1], (HALF_TP, HALF_TP)) for k in range(2)]
    down = [x.T for x in across]
    item = [2 * lax.broadcasted_iota(jnp.int32, (HALF_TP, HALF_TP), 0) + k for k in range(2)]

    def latest(matches):
        found = [
            jnp.max(jnp.where(match, item[k], -1), 0, keepdims=True)
            for k, match in enumerate(matches)
        ]
        found = jnp.maximum(found[0], found[1])
        return jnp.where(found < 0, NJ, found)

    links = []
    for k in range(2):
        here = 2 * lane + k
        links.append(
            latest([jnp.logical_and(down[n] == across[k], item[n] < here) for n in range(2)])
        )
    for half in range(2):
        links.append(latest([down[n] == lane + HALF_TP * half for n in range(2)]))
    return links


def within(entry):
    return jnp.minimum(jnp.maximum(entry, 0), NJ)


CHUNKS = 4
CHUNK_J = 2
GROUP_J = CHUNKS * CHUNK_J


def whole_kernel(
    list_smem, list_vmem, v_hbm, ct_hbm, pt_hbm, cs_hbm, ps_hbm,
    response_hbm, twist_hbm, table_hbm,
    filtered_ref, gradient_ref,
    v_ref, ct_ref, pt_ref, cs_ref, ps_ref, response_ref, twist_ref, table_ref,
    links_vmem, links, gain_ref, stage, arrived0, arrived1, owned, rows0, rows1,
    ready, filtered0, filtered1, picked, returned,
    load_sem, links_sem, out_sem, send_tile, recv_tile, own_tile,
    send_row, recv_row0, recv_row1, own_row, send_out, recv_out, own_out,
    send_pick, recv_pick, own_pick,
):
    loads = [
        pltpu.make_async_copy(source, target, load_sem.at[n])
        for n, (source, target) in enumerate(
            [
                (cs_hbm, cs_ref),
                (ps_hbm, ps_ref),
                (v_hbm, v_ref),
                (ct_hbm, ct_ref),
                (pt_hbm, pt_ref),
                (response_hbm, response_ref),
                (twist_hbm, twist_ref),
                (table_hbm, table_ref),
            ]
        )
    ]
    for load in loads:
        load.start()
    here = Place()
    barrier = greet(here)
    column_me, part_me = here.column, here.part
    me = column_me * TILES + part_me
    arrived, filtered = (arrived0, arrived1), (filtered0, filtered1)
    others = COLS * TILES - 1

    def each_other(step, n, action):
        column = here.target(step, n)
        for dx, part in zip(FAR_FIRST, here.parts):
            send = functools.partial(action, column, part)
            if dx:
                send()
            else:
                unless_self(step, n, send)

    def each_column(action):
        def visit(step, carry):
            for n in range(4):
                unless_self(step, n, functools.partial(action, here.target(step, n)))
            return carry

        lax.fori_loop(0, STEPS, visit, 0)

    def remote(source, target, sent, received, column, part):
        pltpu.make_async_remote_copy(
            source, target, sent, received, device_id=(column, part), device_id_type=MESH
        ).start()

    def compute(half, step):
        for n in range(4):
            column = here.target(step, n)
            for k in range(2):
                slot = 2 * column + k
                row = pl.ds(slot, 1)
                tile = spread_tile(
                    half, v_ref[row, :], ct_ref[slot], pt_ref[slot], cs_ref[row, :], ps_ref[row, :]
                )
                stage[half, pl.ds(column * TILES, TILES), k] = tile.reshape(TILES, 8, HALF_TP)

    def dispatch(half, step, members):
        def send(column, part):
            remote(
                stage.at[half, column * TILES + part],
                arrived[half].at[pl.ds(2 * me, 2)],
                send_tile,
                recv_tile.at[half],
                column,
                part,
            )

        for n in members:
            each_other(step, n, send)

    def own_tiles(half):
        return pltpu.make_async_copy(
            stage.at[half, me], arrived[half].at[pl.ds(2 * me, 2)], own_tile.at[half]
        )

    for load in loads[:5]:
        load.wait()
    compute(0, 0)
    pl.semaphore_wait(barrier, others)
    dispatch(0, 0, (0, 1, 2))
    for half in range(2):

        def spread_step(step, carry):
            compute(half, step)
            dispatch(half, step - 1, (3,))
            dispatch(half, step, (0, 1, 2))
            return carry

        if half:
            compute(half, 0)
            dispatch(0, STEPS - 1, (3,))
            dispatch(1, 0, (0, 1, 2))
            own_tiles(0).start()
        lax.fori_loop(1, STEPS, spread_step, 0)

    for n, link in enumerate(same_block_links(list_vmem[column_me])):
        links_vmem[n : n + 1, :] = link
    dispatch(1, STEPS - 1, (3,))
    own_tiles(1).start()
    for half in range(2):
        arrived[half][NJ] = jnp.zeros((8, HALF_TP), F32)
    loads[5].wait()
    gain_ref[...] = gain_table(response_ref)
    copy_links = pltpu.make_async_copy(links_vmem, links, links_sem)
    copy_links.start()
    copy_links.wait()

    for half in range(2):
        tiles = arrived[half]
        bytes_of(tiles.at[pl.ds(0, 2 * others)], recv_tile.at[half]).wait()
        own_tiles(half).wait()

        def add(b, carry):
            for k in range(2):
                tiles[2 * b + k] = tiles[2 * b + k] + tiles[within(links[k, b])]
            return carry

        lax.fori_loop(0, COLS * TILES, add, 0, unroll=4)

        def gather(column):
            first = column // 16
            for j in range(GROUP_J):
                entry = links[2 + first, (column - 16 * first) * GROUP_J + j]
                owned[half, column * GROUP_J + j] = tiles[within(entry)]

        if half == 0:

            def send_rows(column):
                remote(
                    owned.at[0, pl.ds(column * GROUP_J, GROUP_J)],
                    rows0.at[column_me],
                    send_row,
                    recv_row0,
                    column,
                    part_me,
                )

            def row_step(step, carry):
                for n in range(4):
                    gather(here.target(step, n))
                for n in range(4):
                    column = here.target(step - 1, n)
                    unless_self(step - 1, n, functools.partial(send_rows, column))
                return carry

            for n in range(4):
                gather(here.target(0, n))
            lax.fori_loop(1, STEPS, row_step, 0)
            for n in range(4):
                send_rows(here.target(STEPS - 1, n))
        else:

            def row_step(step, carry):
                for n in range(4):
                    gather(here.target(step, n))
                return carry

            lax.fori_loop(0, STEPS, row_step, 0)

            def send_chunk(chunk, carry):
                def send(column):
                    remote(
                        owned.at[1, pl.ds(column * GROUP_J + chunk * CHUNK_J, CHUNK_J)],
                        rows1.at[chunk, column_me],
                        send_row,
                        recv_row1.at[chunk],
                        column,
                        part_me,
                    )

                each_column(send)
                return carry

            lax.fori_loop(0, CHUNKS, send_chunk, 0)

    own_rows = [
        pltpu.make_async_copy(
            owned.at[0, pl.ds(column_me * GROUP_J, GROUP_J)], rows0.at[column_me], own_row.at[0]
        )
    ]
    for chunk in range(CHUNKS):
        own_rows.append(
            pltpu.make_async_copy(
                owned.at[1, pl.ds(column_me * GROUP_J + chunk * CHUNK_J, CHUNK_J)],
                rows1.at[chunk, column_me],
                own_row.at[1 + chunk],
            )
        )
    for copy in own_rows:
        copy.start()
    for copy in own_rows:
        copy.wait()
    bytes_of(rows0.at[pl.ds(0, COLS - 1)], recv_row0).wait()
    for load in loads[6:]:
        load.wait()

    def chunk_rows(chunk):
        return pl.ds(column_me * GROUP_J + chunk * CHUNK_J, CHUNK_J)

    def own_ready(half, chunk):
        return pltpu.make_async_copy(
            ready.at[half, chunk, column_me],
            filtered[half].at[chunk_rows(chunk)],
            own_out.at[half, chunk],
        )

    def send_ready(half, chunk):
        def send(column):
            remote(
                ready.at[half, chunk, column],
                filtered[half].at[chunk_rows(chunk)],
                send_out,
                recv_out.at[half],
                column,
                part_me,
            )

        each_column(send)
        own_ready(half, chunk).start()

    def filter_chunk(chunk, carry):
        bytes_of(rows1.at[chunk, pl.ds(0, COLS - 1)], recv_row1.at[chunk]).wait()
        rows = []
        for q in range(COLS):
            left = rows0[q, pl.ds(chunk * CHUNK_J, CHUNK_J)].reshape(CHUNK_J * 8, HALF_TP)
            right = rows1[chunk, q].reshape(CHUNK_J * 8, HALF_TP)
            rows.append(jnp.concatenate([left, right], 1))
        rows = filter_rows(rows, gain_ref, twist_ref, [table_ref[n] for n in range(4)])
        for q in range(COLS):
            for half in range(2):
                piece = rows[q][:, half * HALF_TP : (half + 1) * HALF_TP]
                ready[half, chunk, q] = piece.reshape(CHUNK_J, 8, HALF_TP)

        @pl.when(chunk >= 2)
        def _():
            send_ready(1, chunk - 2)

        send_ready(0, chunk)
        return carry

    lax.fori_loop(0, CHUNKS, filter_chunk, 0)
    for chunk in range(CHUNKS - 2, CHUNKS):
        send_ready(1, chunk)

    for half in range(2):
        source = filtered[half]
        for chunk in range(CHUNKS):
            own_ready(half, chunk).wait()
        bytes_of(source.at[pl.ds(0, NJ - GROUP_J)], recv_out.at[half]).wait()
        pltpu.make_async_copy(
            source, filtered_ref.at[:, :, pl.ds(half * HALF_TP, HALF_TP)], out_sem.at[half]
        ).start()

        def pick(step):
            for n in range(4):
                column = here.target(step, n)
                for part in range(TILES):
                    block = column * TILES + part
                    for k in range(2):
                        picked[half, block, k] = source[list_smem[column_me, k, block]]

        def send_picked(column, part):
            remote(
                picked.at[half, column * TILES + part],
                returned.at[half, column_me, part_me],
                send_pick,
                recv_pick.at[half, column_me],
                column,
                part,
            )

        def pick_step(step, carry):
            pick(step)
            for n in range(4):
                each_other(step - 1, n, send_picked)
            return carry

        pick(0)
        lax.fori_loop(1, STEPS, pick_step, 0)
        for n in range(4):
            each_other(STEPS - 1, n, send_picked)
        own = pltpu.make_async_copy(
            picked.at[half, me], returned.at[half, column_me, part_me], own_pick.at[half]
        )
        own.start()
        own.wait()

    def read(step, carry):
        columns = [here.source(step, n) for n in range(4)]
        for column in columns:
            for half in range(2):

                @pl.when(column != column_me)
                def _():
                    bytes_of(returned.at[half, column], recv_pick.at[half, column]).wait()

                @pl.when(column == column_me)
                def _():
                    bytes_of(
                        returned.at[half, column, pl.ds(0, TILES - 1)], recv_pick.at[half, column]
                    ).wait()

        for column in columns:
            for k in range(2):
                slot = 2 * column + k
                row = pl.ds(slot, 1)
                sides = [returned[half, column, :, k].reshape(TR, HALF_TP) for half in range(2)]
                gradient_ref[row, :] = read_tile(
                    jnp.concatenate(sides, 1),
                    ct_ref[slot],
                    pt_ref[slot],
                    cs_ref[row, :],
                    ps_ref[row, :],
                )
        return carry

    lax.fori_loop(0, STEPS, read, 0)
    bytes_of(stage.at[:, pl.ds(0, others)], send_tile).wait()
    bytes_of(owned.at[:, pl.ds(0, NJ - GROUP_J)], send_row).wait()
    bytes_of(ready.at[:, :, pl.ds(0, COLS - 1)], send_out).wait()
    bytes_of(picked.at[:, pl.ds(0, others)], send_pick).wait()
    for half in range(2):
        pltpu.make_async_copy(
            filtered[half],
            filtered_ref.at[:, :, pl.ds(half * HALF_TP, HALF_TP)],
            out_sem.at[half],
        ).wait()


PIECES = 4


def finish_kernel(filtered_in, gradient_in, filtered_out, gradient_out, tiles, points, into, outof):
    def pieces(source, target, sem):
        rows = NJ // PIECES
        copies = [pltpu.make_async_copy(source[1], target[1], sem.at[PIECES])]
        for n in range(PIECES):
            part = pl.ds(n * rows, rows)
            copies.append(
                pltpu.make_async_copy(source[0].at[part], target[0].at[part], sem.at[n])
            )
        return copies

    staged = (tiles, points)
    first = pieces((filtered_in, gradient_in), staged, into)
    second = pieces(staged, (filtered_out, gradient_out), outof)
    for copy in first:
        copy.start()
    for arrival, departure in zip(first, second):
        arrival.wait()
        departure.start()
    for copy in second:
        copy.wait()


def finish(filtered, gradient):
    anywhere = pl.BlockSpec(memory_space=pl.ANY)
    shapes = tuple(jax.ShapeDtypeStruct(x.shape, F32) for x in (filtered, gradient))
    return pl.pallas_call(
        finish_kernel,
        in_specs=[anywhere] * 2,
        out_specs=(anywhere,) * 2,
        out_shape=shapes,
        scratch_shapes=[pltpu.VMEM(x.shape, F32) for x in (filtered, gradient)]
        + [pltpu.SemaphoreType.DMA((PIECES + 1,))] * 2,
        name="finish",
    )(filtered, gradient)


def per_device(values, cycle_taps, phi_taps, cycle_start, phi_start, tile_list, response):
    lists = jnp.transpose(tile_list, (1, 2, 0))
    twist, tables = filter_tables()
    vmem = pl.BlockSpec(memory_space=pltpu.VMEM)
    hbm = pl.BlockSpec(memory_space=pltpu.HBM)
    tile = (8, HALF_TP)
    dma = pltpu.SemaphoreType.DMA
    filtered, gradient = pl.pallas_call(
        whole_kernel,
        in_specs=[pl.BlockSpec(memory_space=pltpu.SMEM), vmem] + [hbm] * 8,
        out_specs=(pl.BlockSpec(memory_space=pl.ANY), vmem),
        out_shape=(
            jax.ShapeDtypeStruct((NJ, 8, TP), F32),
            jax.ShapeDtypeStruct((SLOTS_DEV, PPS), F32),
        ),
        scratch_shapes=[
            pltpu.VMEM(values.shape[1:], F32),
            pltpu.VMEM(cycle_taps.shape[1:], F32),
            pltpu.VMEM(phi_taps.shape[1:], F32),
            pltpu.VMEM(cycle_start.shape[1:], jnp.int32),
            pltpu.VMEM(phi_start.shape[1:], jnp.int32),
            pltpu.VMEM(response.shape, F32),
            pltpu.VMEM(twist.shape, F32),
            pltpu.VMEM(tables.shape, BF16),
            pltpu.VMEM((8, HALF_TP), jnp.int32),
            pltpu.SMEM((8, HALF_TP), jnp.int32),
            pltpu.VMEM((HALF, TP), F32),
            pltpu.VMEM((2, COLS * TILES, 2) + tile, F32),
            pltpu.VMEM((NJ + 2,) + tile, F32),
            pltpu.VMEM((NJ + 2,) + tile, F32),
            pltpu.VMEM((2, NJ) + tile, F32),
            pltpu.VMEM((COLS, GROUP_J) + tile, F32),
            pltpu.VMEM((CHUNKS, COLS, CHUNK_J) + tile, F32),
            pltpu.VMEM((2, CHUNKS, COLS, CHUNK_J) + tile, F32),
            pltpu.VMEM((NJ,) + tile, F32),
            pltpu.VMEM((NJ,) + tile, F32),
            pltpu.VMEM((2, COLS * TILES, 2) + tile, F32),
            pltpu.VMEM((2, COLS, TILES, 2) + tile, F32),
            dma((8,)),
            dma,
            dma((2,)),
            dma,
            dma((2,)),
            dma((2,)),
            dma,
            dma,
            dma((CHUNKS,)),
            dma((1 + CHUNKS,)),
            dma,
            dma((2,)),
            dma((2, CHUNKS)),
            dma,
            dma((2, COLS)),
            dma((2,)),
        ],
        compiler_params=pltpu.CompilerParams(
            collective_id=0, has_side_effects=True, vmem_limit_bytes=57 << 20
        ),
        name="whole",
    )(
        lists,
        lists,
        values[0],
        cycle_taps[0],
        phi_taps[0],
        cycle_start[0],
        phi_start[0],
        response,
        jnp.asarray(twist),
        jnp.asarray(tables),
    )
    filtered, gradient = finish(filtered, gradient)
    return filtered, gradient[None]


def solution(mesh):
    return jax.shard_map(
        per_device,
        mesh=mesh,
        in_specs=(
            P(("pts", "tile"), None, None),
            P(("pts", "tile"), None, None, None),
            P(("pts", "tile"), None, None, None),
            P(("pts", "tile"), None, None),
            P(("pts", "tile"), None, None),
            P(),
            P(),
        ),
        out_specs=(P(None, "tile", "pts"), P(("pts", "tile"), None, None)),
        check_vma=False,
    )
```

```python
import functools
import math

import jax
import jax.numpy as jnp
import numpy as np
from jax import lax
from jax.experimental import pallas as pl
from jax.experimental.pallas import tpu as pltpu
from jax.sharding import PartitionSpec as P

NPHI = 8192
TR = 32
NJ = 256
TP = 256
PPS = 1024
COLS = 32
SLOTS_DEV = 64
HALF = COLS // 2 + 1
HALF_TP = TP // 2

F32 = jnp.float32
BF16 = jnp.bfloat16
CONTRACT_LAST = (((1,), (1,)), ((), ()))


def split(x):
    high = x.astype(BF16)
    return high, (x - high.astype(F32)).astype(BF16)


def place(taps, start):
    count = taps.shape[1]
    row = lax.broadcasted_iota(jnp.int32, (8, count), 0)
    starts = jnp.broadcast_to(start, (8, count))
    for bit in (1, 2, 4):
        taps = jnp.where((starts & bit) != 0, pltpu.roll(taps, bit, 0), taps)
    return taps, (starts - row + 7) >> 3


def expand(parts, group, groups, first=0):
    group = group.astype(F32)
    count = group.shape[1]
    pair = jnp.concatenate([group, group - 1.0], 0).astype(BF16)
    doubled = [jnp.concatenate([part.astype(F32)] * 2, 0).astype(BF16) for part in parts]
    zero = jnp.zeros((16, count), BF16)
    rows = [[] for _ in parts]
    for index in range(groups // 2):
        mask = pair == jnp.asarray(2 * index + first, BF16)
        for out, part in zip(rows, doubled):
            out.append(jnp.where(mask, part, zero))
    return [jnp.concatenate(out, 0) for out in rows]


MESH = pl.DeviceIdType.MESH
TILES = 4
FAR_FIRST = (2, 1, 3, 0)
STEPS = COLS // 4
SELF_STEP = 5


def spread_tile(half, values, cycle_taps, phi_taps, cycle_start, phi_start):
    cycle, cycle_group = place(cycle_taps * values, cycle_start)
    phi, phi_group = place(phi_taps, phi_start)
    cycle_high, cycle_low = expand(split(cycle), cycle_group, TR // 8)
    phi_high, phi_low = expand(split(phi), phi_group, HALF_TP // 8, half * (HALF_TP // 8))
    stacked = jnp.concatenate([cycle_high, cycle_low], 0)
    first = lax.dot_general(phi_high, stacked, CONTRACT_LAST, preferred_element_type=F32)
    second = lax.dot_general(phi_low, cycle_high, CONTRACT_LAST, preferred_element_type=F32)
    return (first[:, :TR] + first[:, TR:] + second).T


def read_tile(tile, cycle_taps, phi_taps, cycle_start, phi_start):
    tile_high, tile_low = split(tile)
    cycle, cycle_group = place(cycle_taps, cycle_start)
    phi, phi_group = place(phi_taps, phi_start)
    cycle_high, cycle_low = expand(split(cycle), cycle_group, TR // 8)
    right = jnp.concatenate([cycle_high, cycle_low, cycle_high], 0)
    left = jnp.concatenate([tile_high, tile_high, tile_low], 0).T
    along = jnp.dot(left, right, preferred_element_type=F32)
    picked = jnp.zeros((8, PPS), F32)
    for g in range(TP // 8):
        picked = jnp.where(phi_group == g, along[8 * g : 8 * g + 8], picked)
    return jnp.sum(picked * phi, 0, keepdims=True)


class Place:
    def __init__(self):
        self.column = lax.axis_index("pts")
        self.part = lax.axis_index("tile")
        z, self.y = self.column // 8, lax.rem(self.column // 2, 4)
        self.core = lax.rem(self.column, 2)
        self.ahead = [lax.rem(z + dz, 4) * 8 for dz in FAR_FIRST]
        self.behind = [lax.rem(z + 4 - dz, 4) * 8 for dz in FAR_FIRST]
        self.parts = [lax.rem(self.part + dx, 4) for dx in FAR_FIRST]

    def core_at(self, step):
        return lax.rem(self.core + 1 + step // 4, 2)

    def target(self, step, n):
        return self.ahead[n] + 2 * lax.rem(self.y + step + n, 4) + self.core_at(step)

    def source(self, step, n):
        return self.behind[n] + 2 * lax.rem(self.y + 16 - step - n, 4) + self.core_at(step)


def unless_self(step, n, action):
    if n != 3:
        action()
    elif isinstance(step, int):
        if step != SELF_STEP:
            action()
    else:
        pl.when(step != SELF_STEP)(action)


def greet(here):
    barrier = pltpu.get_barrier_semaphore()
    for step in range(STEPS):
        for n in range(4):
            column = here.target(step, n)
            for dx, part in zip(FAR_FIRST, here.parts):
                if (step, n, dx) != (SELF_STEP, 3, 0):
                    pl.semaphore_signal(
                        barrier, inc=1, device_id=(column, part), device_id_type=MESH
                    )
    return barrier


def bytes_of(ref, sem):
    return pltpu.make_async_copy(ref, ref, sem)


def times(re, im, cos, sin):
    return re * cos - im * sin, re * sin + im * cos


def turn(re, im, angle):
    cos, sin = math.cos(angle), math.sin(angle)
    if abs(sin) < 1e-12:
        return (re, im) if cos > 0 else (-re, -im)
    if abs(cos) < 1e-12:
        return (-im, re) if sin > 0 else (im, -re)
    return re * cos - im * sin, re * sin + im * cos


def real_fft(x):
    n = len(x)
    if n == 1:
        return [(x[0], None)]
    if n == 2:
        return [(x[0] + x[1], None), (x[0] - x[1], None)]
    even, odd = real_fft(x[0::2]), real_fft(x[1::2])
    out = [None] * (n // 2 + 1)
    out[0] = (even[0][0] + odd[0][0], None)
    out[n // 2] = (even[0][0] - odd[0][0], None)
    for k in range(1, n // 4):
        er, ei = even[k]
        tr, ti = turn(odd[k][0], odd[k][1], -2.0 * math.pi * k / n)
        out[k] = (er + tr, ei + ti)
        out[n // 2 - k] = (er - tr, ti - ei)
    quarter = n // 4
    out[quarter] = (even[quarter][0], -odd[quarter][0])
    return out


def real_inverse(spec):
    half = len(spec) - 1
    n = 2 * half
    if n == 2:
        return [spec[0][0] + spec[1][0], spec[0][0] - spec[1][0]]
    even, odd = [None] * (half // 2 + 1), [None] * (half // 2 + 1)
    even[0] = (spec[0][0] + spec[half][0], None)
    odd[0] = (spec[0][0] - spec[half][0], None)
    for k in range(1, half // 2):
        ar, ai = spec[k]
        br, bi = spec[half - k]
        even[k] = (ar + br, ai - bi)
        odd[k] = turn(ar - br, ai + bi, 2.0 * math.pi * k / n)
    middle = half // 2
    even[middle] = (2.0 * spec[middle][0], None)
    odd[middle] = (-2.0 * spec[middle][1], None)
    out = [None] * n
    out[0::2] = real_inverse(even)
    out[1::2] = real_inverse(odd)
    return out


def times_table(rows, table_high, table_low):
    high, low = split(rows)
    dot = functools.partial(jnp.dot, preferred_element_type=F32)
    return dot(high, table_high) + dot(high, table_low) + dot(low, table_high)


def filter_rows(rows, gain_ref, twist_ref, tables):
    cycles = rows[0].shape[0]
    spec = real_fft(rows)
    reals, imags = [], []
    for k in range(HALF):
        cos, sin = twist_ref[0, k : k + 1, :], twist_ref[1, k : k + 1, :]
        re, im = spec[k]
        if im is None:
            reals.append(re * cos)
            imags.append(-re * sin)
        else:
            re, im = times(re, im, cos, -sin)
            reals.append(re)
            imags.append(im)
    count = HALF * cycles
    both = times_table(jnp.concatenate(reals + imags, 0), tables[0], tables[1])
    first, last = both[:count], both[count:]
    freq_re = first[:, :TP] + last[:, TP:]
    freq_im = last[:, :TP] - first[:, TP:]
    gains = [jnp.broadcast_to(gain_ref[k : k + 1, :], (cycles, TP)) for k in range(HALF)]
    gain = jnp.concatenate(gains, 0)
    both = times_table(
        jnp.concatenate([freq_re * gain, freq_im * gain], 0), tables[2], tables[3]
    )
    first, last = both[:count], both[count:]
    back_re = first[:, :TP] - last[:, TP:]
    back_im = last[:, :TP] + first[:, TP:]
    spec = []
    for k in range(HALF):
        cos, sin = twist_ref[0, k : k + 1, :], twist_ref[1, k : k + 1, :]
        re, im = back_re[k * cycles : (k + 1) * cycles], back_im[k * cycles : (k + 1) * cycles]
        spec.append(times(re, im, cos, sin))
    return real_inverse(spec)


def filter_tables():
    index = np.arange(TP)
    low_half = 4 * (np.arange(HALF_TP) % COLS) + np.arange(HALF_TP) // COLS
    order = np.concatenate([low_half, TP - 1 - low_half])
    angle = 2.0 * np.pi * (np.outer(index, order) % TP) / TP
    tables = []
    for cos, sin in [(np.cos(angle), np.sin(angle)), (np.cos(angle).T, np.sin(angle).T)]:
        table = np.concatenate([cos, sin], 1).astype(np.float32)
        high = table.astype(BF16)
        tables += [high, (table - high.astype(np.float32)).astype(BF16)]
    angle = 2.0 * np.pi * np.outer(np.arange(HALF), index) / NPHI
    return np.stack([np.cos(angle), np.sin(angle)]).astype(np.float32), np.stack(tables)


def gain_table(response_ref):
    rows = [response_ref[HALF_TP * s : HALF_TP * (s + 1)].reshape(1, HALF_TP) for s in range(COLS)]
    turned = jnp.concatenate(rows, 0).T
    grid = jnp.concatenate([turned[COLS * b : COLS * (b + 1)] for b in range(4)], 1)
    lane = lax.broadcasted_iota(jnp.int32, (8, HALF_TP), 1)
    zeroth = jnp.broadcast_to(grid[:1], (8, HALF_TP))
    ahead = jnp.where(
        lane < 3 * COLS, pltpu.roll(zeroth, 3 * COLS, 1), pltpu.roll(zeroth, 3 * COLS - 1, 1)
    )
    last = response_ref[NPHI // 2 : NPHI // 2 + 1].reshape(1, 1)
    ahead = jnp.where(lane == HALF_TP - 1, jnp.broadcast_to(last, (8, HALF_TP)), ahead)
    mirrored = [ahead[:1]] + [grid[COLS - k : COLS - k + 1] for k in range(1, HALF)]
    both = jnp.concatenate([grid[:HALF], jnp.concatenate(mirrored, 0)], 1)
    return both * (1.0 / NPHI)


def same_block_links(wanted):
    lane = lax.broadcasted_iota(jnp.int32, (HALF_TP, HALF_TP), 1)
    across = [jnp.broadcast_to(wanted[k : k + 1], (HALF_TP, HALF_TP)) for k in range(2)]
    down = [x.T for x in across]
    item = [2 * lax.broadcasted_iota(jnp.int32, (HALF_TP, HALF_TP), 0) + k for k in range(2)]

    def latest(matches):
        found = [
            jnp.max(jnp.where(match, item[k], -1), 0, keepdims=True)
            for k, match in enumerate(matches)
        ]
        found = jnp.maximum(found[0], found[1])
        return jnp.where(found < 0, NJ, found)

    links = []
    for k in range(2):
        here = 2 * lane + k
        links.append(
            latest([jnp.logical_and(down[n] == across[k], item[n] < here) for n in range(2)])
        )
    for half in range(2):
        links.append(latest([down[n] == lane + HALF_TP * half for n in range(2)]))
    return links


def within(entry):
    return jnp.minimum(jnp.maximum(entry, 0), NJ)


CHUNKS = 4
CHUNK_J = 2
GROUP_J = CHUNKS * CHUNK_J


def whole_kernel(
    list_smem, list_vmem, v_hbm, ct_hbm, pt_hbm, cs_hbm, ps_hbm,
    response_hbm, twist_hbm, table_hbm,
    filtered_ref, gradient_ref,
    v_ref, ct_ref, pt_ref, cs_ref, ps_ref, response_ref, twist_ref, table_ref,
    links_vmem, links, gain_ref, stage, arrived0, arrived1, owned, rows0, rows1,
    ready, filtered0, filtered1, picked, returned,
    load_sem, links_sem, out_sem, send_tile, recv_tile, own_tile,
    send_row, recv_row0, recv_row1, own_row, send_out, recv_out, own_out,
    send_pick, recv_pick, own_pick,
):
    loads = [
        pltpu.make_async_copy(source, target, load_sem.at[n])
        for n, (source, target) in enumerate(
            [
                (cs_hbm, cs_ref),
                (ps_hbm, ps_ref),
                (v_hbm, v_ref),
                (ct_hbm, ct_ref),
                (pt_hbm, pt_ref),
                (response_hbm, response_ref),
                (twist_hbm, twist_ref),
                (table_hbm, table_ref),
            ]
        )
    ]
    for load in loads:
        load.start()
    here = Place()
    barrier = greet(here)
    column_me, part_me = here.column, here.part
    me = column_me * TILES + part_me
    arrived, filtered = (arrived0, arrived1), (filtered0, filtered1)
    others = COLS * TILES - 1

    def each_other(step, n, action):
        column = here.target(step, n)
        for dx, part in zip(FAR_FIRST, here.parts):
            send = functools.partial(action, column, part)
            if dx:
                send()
            else:
                unless_self(step, n, send)

    def each_column(action):
        def visit(step, carry):
            for n in range(4):
                unless_self(step, n, functools.partial(action, here.target(step, n)))
            return carry

        lax.fori_loop(0, STEPS, visit, 0)

    def remote(source, target, sent, received, column, part):
        pltpu.make_async_remote_copy(
            source, target, sent, received, device_id=(column, part), device_id_type=MESH
        ).start()

    for n, link in enumerate(same_block_links(list_vmem[column_me])):
        links_vmem[n : n + 1, :] = link
    for load in loads[:6]:
        load.wait()
    gain_ref[...] = gain_table(response_ref)
    for half in range(2):
        arrived[half][NJ] = jnp.zeros((8, HALF_TP), F32)

    def compute(half, step):
        for n in range(4):
            column = here.target(step, n)
            for k in range(2):
                slot = 2 * column + k
                row = pl.ds(slot, 1)
                tile = spread_tile(
                    half, v_ref[row, :], ct_ref[slot], pt_ref[slot], cs_ref[row, :], ps_ref[row, :]
                )
                stage[half, pl.ds(column * TILES, TILES), k] = tile.reshape(TILES, 8, HALF_TP)

    def dispatch(half, step):
        def send(column, part):
            remote(
                stage.at[half, column * TILES + part],
                arrived[half].at[pl.ds(2 * me, 2)],
                send_tile,
                recv_tile.at[half],
                column,
                part,
            )

        for n in range(4):
            each_other(step, n, send)

    def own_tiles(half):
        return pltpu.make_async_copy(
            stage.at[half, me], arrived[half].at[pl.ds(2 * me, 2)], own_tile.at[half]
        )

    copy_links = pltpu.make_async_copy(links_vmem, links, links_sem)
    compute(0, 0)
    copy_links.start()
    pl.semaphore_wait(barrier, others)
    for half in range(2):

        def spread_step(step, carry):
            compute(half, step)
            dispatch(half, step - 1)
            return carry

        if half:
            compute(half, 0)
            dispatch(0, STEPS - 1)
            own_tiles(0).start()
        lax.fori_loop(1, STEPS, spread_step, 0)
    dispatch(1, STEPS - 1)
    own_tiles(1).start()
    copy_links.wait()

    for half in range(2):
        tiles = arrived[half]
        bytes_of(tiles.at[pl.ds(0, 2 * others)], recv_tile.at[half]).wait()
        own_tiles(half).wait()

        def add(b, carry):
            for k in range(2):
                tiles[2 * b + k] = tiles[2 * b + k] + tiles[within(links[k, b])]
            return carry

        lax.fori_loop(0, COLS * TILES, add, 0, unroll=4)

        def gather(column):
            first = column // 16
            for j in range(GROUP_J):
                entry = links[2 + first, (column - 16 * first) * GROUP_J + j]
                owned[half, column * GROUP_J + j] = tiles[within(entry)]

        if half == 0:

            def send_rows(column):
                remote(
                    owned.at[0, pl.ds(column * GROUP_J, GROUP_J)],
                    rows0.at[column_me],
                    send_row,
                    recv_row0,
                    column,
                    part_me,
                )

            def row_step(step, carry):
                for n in range(4):
                    gather(here.target(step, n))
                for n in range(4):
                    column = here.target(step - 1, n)
                    unless_self(step - 1, n, functools.partial(send_rows, column))
                return carry

            for n in range(4):
                gather(here.target(0, n))
            lax.fori_loop(1, STEPS, row_step, 0)
            for n in range(4):
                send_rows(here.target(STEPS - 1, n))
        else:

            def row_step(step, carry):
                for n in range(4):
                    gather(here.target(step, n))
                return carry

            lax.fori_loop(0, STEPS, row_step, 0)

            def send_chunk(chunk, carry):
                def send(column):
                    remote(
                        owned.at[1, pl.ds(column * GROUP_J + chunk * CHUNK_J, CHUNK_J)],
                        rows1.at[chunk, column_me],
                        send_row,
                        recv_row1.at[chunk],
                        column,
                        part_me,
                    )

                each_column(send)
                return carry

            lax.fori_loop(0, CHUNKS, send_chunk, 0)

    own_rows = [
        pltpu.make_async_copy(
            owned.at[0, pl.ds(column_me * GROUP_J, GROUP_J)], rows0.at[column_me], own_row.at[0]
        )
    ]
    for chunk in range(CHUNKS):
        own_rows.append(
            pltpu.make_async_copy(
                owned.at[1, pl.ds(column_me * GROUP_J + chunk * CHUNK_J, CHUNK_J)],
                rows1.at[chunk, column_me],
                own_row.at[1 + chunk],
            )
        )
    for copy in own_rows:
        copy.start()
    for copy in own_rows:
        copy.wait()
    bytes_of(rows0.at[pl.ds(0, COLS - 1)], recv_row0).wait()
    for load in loads[6:]:
        load.wait()

    def chunk_rows(chunk):
        return pl.ds(column_me * GROUP_J + chunk * CHUNK_J, CHUNK_J)

    def own_ready(half, chunk):
        return pltpu.make_async_copy(
            ready.at[half, chunk, column_me],
            filtered[half].at[chunk_rows(chunk)],
            own_out.at[half, chunk],
        )

    def send_ready(half, chunk):
        def send(column):
            remote(
                ready.at[half, chunk, column],
                filtered[half].at[chunk_rows(chunk)],
                send_out,
                recv_out.at[half],
                column,
                part_me,
            )

        each_column(send)
        own_ready(half, chunk).start()

    def filter_chunk(chunk, carry):
        bytes_of(rows1.at[chunk, pl.ds(0, COLS - 1)], recv_row1.at[chunk]).wait()
        rows = []
        for q in range(COLS):
            left = rows0[q, pl.ds(chunk * CHUNK_J, CHUNK_J)].reshape(CHUNK_J * 8, HALF_TP)
            right = rows1[chunk, q].reshape(CHUNK_J * 8, HALF_TP)
            rows.append(jnp.concatenate([left, right], 1))
        rows = filter_rows(rows, gain_ref, twist_ref, [table_ref[n] for n in range(4)])
        for q in range(COLS):
            for half in range(2):
                piece = rows[q][:, half * HALF_TP : (half + 1) * HALF_TP]
                ready[half, chunk, q] = piece.reshape(CHUNK_J, 8, HALF_TP)

        @pl.when(chunk >= 2)
        def _():
            send_ready(1, chunk - 2)

        send_ready(0, chunk)
        return carry

    lax.fori_loop(0, CHUNKS, filter_chunk, 0)
    for chunk in range(CHUNKS - 2, CHUNKS):
        send_ready(1, chunk)

    for half in range(2):
        source = filtered[half]
        for chunk in range(CHUNKS):
            own_ready(half, chunk).wait()
        bytes_of(source.at[pl.ds(0, NJ - GROUP_J)], recv_out.at[half]).wait()
        pltpu.make_async_copy(
            source, filtered_ref.at[:, :, pl.ds(half * HALF_TP, HALF_TP)], out_sem.at[half]
        ).start()

        def pick(step):
            for n in range(4):
                column = here.target(step, n)
                for part in range(TILES):
                    block = column * TILES + part
                    for k in range(2):
                        picked[half, block, k] = source[list_smem[column_me, k, block]]

        def send_picked(column, part):
            remote(
                picked.at[half, column * TILES + part],
                returned.at[half, column_me, part_me],
                send_pick,
                recv_pick.at[half, column_me],
                column,
                part,
            )

        def pick_step(step, carry):
            pick(step)
            for n in range(4):
                each_other(step - 1, n, send_picked)
            return carry

        pick(0)
        lax.fori_loop(1, STEPS, pick_step, 0)
        for n in range(4):
            each_other(STEPS - 1, n, send_picked)
        own = pltpu.make_async_copy(
            picked.at[half, me], returned.at[half, column_me, part_me], own_pick.at[half]
        )
        own.start()
        own.wait()

    def read(step, carry):
        columns = [here.source(step, n) for n in range(4)]
        for column in columns:
            for half in range(2):

                @pl.when(column != column_me)
                def _():
                    bytes_of(returned.at[half, column], recv_pick.at[half, column]).wait()

                @pl.when(column == column_me)
                def _():
                    bytes_of(
                        returned.at[half, column, pl.ds(0, TILES - 1)], recv_pick.at[half, column]
                    ).wait()

        for column in columns:
            for k in range(2):
                slot = 2 * column + k
                row = pl.ds(slot, 1)
                sides = [returned[half, column, :, k].reshape(TR, HALF_TP) for half in range(2)]
                gradient_ref[row, :] = read_tile(
                    jnp.concatenate(sides, 1),
                    ct_ref[slot],
                    pt_ref[slot],
                    cs_ref[row, :],
                    ps_ref[row, :],
                )
        return carry

    lax.fori_loop(0, STEPS, read, 0)
    bytes_of(stage.at[:, pl.ds(0, others)], send_tile).wait()
    bytes_of(owned.at[:, pl.ds(0, NJ - GROUP_J)], send_row).wait()
    bytes_of(ready.at[:, :, pl.ds(0, COLS - 1)], send_out).wait()
    bytes_of(picked.at[:, pl.ds(0, others)], send_pick).wait()
    for half in range(2):
        pltpu.make_async_copy(
            filtered[half],
            filtered_ref.at[:, :, pl.ds(half * HALF_TP, HALF_TP)],
            out_sem.at[half],
        ).wait()


PIECES = 4


def finish_kernel(filtered_in, gradient_in, filtered_out, gradient_out, tiles, points, into, outof):
    def pieces(source, target, sem):
        rows = NJ // PIECES
        copies = [pltpu.make_async_copy(source[1], target[1], sem.at[PIECES])]
        for n in range(PIECES):
            part = pl.ds(n * rows, rows)
            copies.append(
                pltpu.make_async_copy(source[0].at[part], target[0].at[part], sem.at[n])
            )
        return copies

    staged = (tiles, points)
    first = pieces((filtered_in, gradient_in), staged, into)
    second = pieces(staged, (filtered_out, gradient_out), outof)
    for copy in first:
        copy.start()
    for arrival, departure in zip(first, second):
        arrival.wait()
        departure.start()
    for copy in second:
        copy.wait()


def finish(filtered, gradient):
    anywhere = pl.BlockSpec(memory_space=pl.ANY)
    shapes = tuple(jax.ShapeDtypeStruct(x.shape, F32) for x in (filtered, gradient))
    return pl.pallas_call(
        finish_kernel,
        in_specs=[anywhere] * 2,
        out_specs=(anywhere,) * 2,
        out_shape=shapes,
        scratch_shapes=[pltpu.VMEM(x.shape, F32) for x in (filtered, gradient)]
        + [pltpu.SemaphoreType.DMA((PIECES + 1,))] * 2,
        name="finish",
    )(filtered, gradient)


def per_device(values, cycle_taps, phi_taps, cycle_start, phi_start, tile_list, response):
    lists = jnp.transpose(tile_list, (1, 2, 0))
    twist, tables = filter_tables()
    vmem = pl.BlockSpec(memory_space=pltpu.VMEM)
    hbm = pl.BlockSpec(memory_space=pltpu.HBM)
    tile = (8, HALF_TP)
    dma = pltpu.SemaphoreType.DMA
    filtered, gradient = pl.pallas_call(
        whole_kernel,
        in_specs=[pl.BlockSpec(memory_space=pltpu.SMEM), vmem] + [hbm] * 8,
        out_specs=(pl.BlockSpec(memory_space=pl.ANY), vmem),
        out_shape=(
            jax.ShapeDtypeStruct((NJ, 8, TP), F32),
            jax.ShapeDtypeStruct((SLOTS_DEV, PPS), F32),
        ),
        scratch_shapes=[
            pltpu.VMEM(values.shape[1:], F32),
            pltpu.VMEM(cycle_taps.shape[1:], F32),
            pltpu.VMEM(phi_taps.shape[1:], F32),
            pltpu.VMEM(cycle_start.shape[1:], jnp.int32),
            pltpu.VMEM(phi_start.shape[1:], jnp.int32),
            pltpu.VMEM(response.shape, F32),
            pltpu.VMEM(twist.shape, F32),
            pltpu.VMEM(tables.shape, BF16),
            pltpu.VMEM((8, HALF_TP), jnp.int32),
            pltpu.SMEM((8, HALF_TP), jnp.int32),
            pltpu.VMEM((HALF, TP), F32),
            pltpu.VMEM((2, COLS * TILES, 2) + tile, F32),
            pltpu.VMEM((NJ + 2,) + tile, F32),
            pltpu.VMEM((NJ + 2,) + tile, F32),
            pltpu.VMEM((2, NJ) + tile, F32),
            pltpu.VMEM((COLS, GROUP_J) + tile, F32),
            pltpu.VMEM((CHUNKS, COLS, CHUNK_J) + tile, F32),
            pltpu.VMEM((2, CHUNKS, COLS, CHUNK_J) + tile, F32),
            pltpu.VMEM((NJ,) + tile, F32),
            pltpu.VMEM((NJ,) + tile, F32),
            pltpu.VMEM((2, COLS * TILES, 2) + tile, F32),
            pltpu.VMEM((2, COLS, TILES, 2) + tile, F32),
            dma((8,)),
            dma,
            dma((2,)),
            dma,
            dma((2,)),
            dma((2,)),
            dma,
            dma,
            dma((CHUNKS,)),
            dma((1 + CHUNKS,)),
            dma,
            dma((2,)),
            dma((2, CHUNKS)),
            dma,
            dma((2, COLS)),
            dma((2,)),
        ],
        compiler_params=pltpu.CompilerParams(
            collective_id=0, has_side_effects=True, vmem_limit_bytes=57 << 20
        ),
        name="whole",
    )(
        lists,
        lists,
        values[0],
        cycle_taps[0],
        phi_taps[0],
        cycle_start[0],
        phi_start[0],
        response,
        jnp.asarray(twist),
        jnp.asarray(tables),
    )
    filtered, gradient = finish(filtered, gradient)
    return filtered, gradient[None]


def solution(mesh):
    return jax.shard_map(
        per_device,
        mesh=mesh,
        in_specs=(
            P(("pts", "tile"), None, None),
            P(("pts", "tile"), None, None, None),
            P(("pts", "tile"), None, None, None),
            P(("pts", "tile"), None, None),
            P(("pts", "tile"), None, None),
            P(),
            P(),
        ),
        out_specs=(P(None, "tile", "pts"), P(("pts", "tile"), None, None)),
        check_vma=False,
    )
```
